32 devices in a mesh: nodes: 8 (over z, y), rep: 4 (over x, core).
Axes of the slice: x: 2, y: 2, z: 4, core: 2. Of those that a mesh axis runs over, the one named last changes fastest.
Arguments:
- features: bfloat16 [16384, 256], P('nodes'), may hold values from -64 to 64
- virtual_state: bfloat16 [4, 256], replicated, may hold values from -64 to 64
- w_query: bfloat16 [256, 256], P(None, 'rep'), may hold values from -0.375 to 0.375
- w_key: bfloat16 [256, 256], P(None, 'rep'), may hold values from -0.375 to 0.375
- w_value: bfloat16 [256, 256], P(None, 'rep'), may hold values from -0.375 to 0.375
- w_out: bfloat16 [256, 256], P('rep'), may hold values from -0.375 to 0.375
- tile_map: int32 [128, 4], P('nodes'), may hold values from 0 to 127, as said below
- local_nbr: int32 [16384, 16], P('nodes'), may hold values from 0 to 127
Outputs:
- node_out: bfloat16 [16384, 256], P('nodes', 'rep')
- virtual_out: bfloat16 [4, 256], P(None, 'rep')
The draws below stay inside these ranges and needn't reach their ends.
Inputs may be any that keep to these rules, and one draw needn't show every extreme that they name: `tile_map`: entry [c, j] is a block number. In the 16 aligned rows of one index e of nodes, the blocks numbered f * 16 to (f + 1) * 16 - 1 are named exactly 16 * 4 / 8 times, for every f.
All inputs are finite; a program needn't handle non-finite values.
Results may differ from the reference program's by a relative error of at most 0.0029.
The reference program's roundings to bfloat16 on the way (of `head_rows` and `virtual_heads`) count: a program that leaves them out, or rounds other values in their place, can miss the bound.
Values may be sent and summed in bfloat16 or wider, within the bound.
A program may use at most 64 MiB of HBM per device.

```python
import math
import jax
import jax.numpy as jnp
from jax import lax

D = 256
H = 8
TILE = 128
DEG = 4
LDEG = 16
G = 4
NB_DEV = 16
NODES = 16384
N_NODES = 8


def draw_features(key, part):
    total_rows = NB_DEV * TILE * N_NODES
    key_one = jax.random.fold_in(key, 0)
    values = jnp.clip(jax.random.normal(key_one, (total_rows, D), jnp.float32), -4.0, 4.0)
    return values.astype(jnp.bfloat16)


def draw_virtual_state(key, part):
    key_one = jax.random.fold_in(key, 0)
    values = jnp.clip(jax.random.normal(key_one, (G, D), jnp.float32), -4.0, 4.0)
    return values.astype(jnp.bfloat16)


def draw_tile_map(key, part):
    key_one, key_two = jax.random.split(key, 2)
    per_peer = NB_DEV * DEG // N_NODES
    owners = jnp.repeat(jnp.arange(N_NODES, dtype=jnp.int32), per_peer)
    device_keys = jax.random.split(key_one, N_NODES)
    shuffled = jax.vmap(lambda single: jax.random.permutation(single, owners))(device_keys)
    within = jax.random.randint(key_two, (N_NODES, NB_DEV * DEG), 0, NB_DEV, jnp.int32)
    return (shuffled * NB_DEV + within).reshape(NB_DEV * N_NODES, DEG)


def plant(values, key, least, high):
    spot = [jax.random.randint(jax.random.fold_in(key, axis), (), 0, length) for axis, length in enumerate(values.shape)]
    main_axis = values.shape.index(max(values.shape))
    neighbour = spot[:main_axis] + [(spot[main_axis] + 1) % values.shape[main_axis]] + spot[main_axis + 1:]
    return values.at[tuple(spot)].set(least).at[tuple(neighbour)].set(high)


def shard_levels(rng, extent, pieces, low, largest):
    factor_of, own = 1.0, jax.random.fold_in(rng, 6)
    for axis_at, blocks in pieces:
        steps = jnp.exp(jax.random.uniform(jax.random.fold_in(own, axis_at), (blocks,), jnp.float32, low / len(pieces), largest / len(pieces)))
        factor_of = factor_of * jnp.repeat(steps, extent[axis_at] // blocks).reshape([-1 if axis == axis_at else 1 for axis in range(len(extent))])
    return factor_of


def centred(key, shape, width, bound, pieces=(), kind=jnp.bfloat16):
    array = width * jax.random.normal(key, shape, jnp.float32)
    if pieces:
        array = array * shard_levels(key, shape, pieces, -0.22, 0.18)
    return jnp.clip(array, -bound, bound).astype(kind)


def setup_inputs(seed: int = 0) -> dict:
    key_of = jax.random.split(jax.random.key(seed), 9)
    features = draw_features(jax.random.fold_in(key_of[8], 71), 0)
    virtual_state = draw_virtual_state(jax.random.fold_in(key_of[8], 71), 0)
    w_query = centred(key_of[2], (D, D), D ** -0.5, 0.375, ((1, 4),))
    w_key = centred(key_of[3], (D, D), D ** -0.5, 0.375, ((1, 4),))
    w_value = centred(key_of[4], (D, D), D ** -0.5, 0.375, ((1, 4),))
    w_out = centred(key_of[5], (D, D), D ** -0.5, 0.375, ((0, 4),))
    tile_map = draw_tile_map(jax.random.fold_in(key_of[8], 71), 0)
    local_nbr = plant(jax.random.randint(key_of[7], (NODES, LDEG), 0, TILE), jax.random.fold_in(key_of[7], 1), 0, TILE - 1).astype(jnp.int32)
    return dict(features=features, virtual_state=virtual_state, w_query=w_query, w_key=w_key, w_value=w_value, w_out=w_out, tile_map=tile_map, local_nbr=local_nbr)


def project(source, weight):
    return jnp.dot(source, weight, preferred_element_type=jnp.float32).astype(jnp.bfloat16)

def reference(features, virtual_state, w_query, w_key, w_value, w_out, tile_map, local_nbr):
    head_size = D // H
    score_scale = 1.0 / math.sqrt(head_size)
    node_count = features.shape[0]
    block_count = node_count // TILE
    queries = project(features, w_query).reshape(block_count, TILE, H, head_size)
    keys_all = project(features, w_key).reshape(block_count, TILE, H, head_size)
    values_all = project(features, w_value).reshape(block_count, TILE, H, head_size)
    virtual_queries = project(virtual_state, w_query).reshape(G, H, head_size)
    virtual_keys = project(virtual_state, w_key).reshape(G, H, head_size)
    virtual_values = project(virtual_state, w_value).reshape(G, H, head_size)
    links = local_nbr.reshape(block_count, TILE, LDEG)
    columns = jnp.arange(TILE, dtype=jnp.int32)

    def attend(block):
        neighbours = tile_map[block]
        key_rows = jnp.concatenate([keys_all[block], keys_all[neighbours].reshape(DEG * TILE, H, head_size), virtual_keys], axis=0)
        value_rows = jnp.concatenate([values_all[block], values_all[neighbours].reshape(DEG * TILE, H, head_size), virtual_values], axis=0)
        scores = jnp.einsum('qhd,khd->hqk', queries[block].astype(jnp.float32), key_rows.astype(jnp.float32), precision=lax.Precision.HIGHEST) * score_scale
        linked = jnp.any(links[block][:, :, None] == columns[None, None, :], axis=1)
        allowed = jnp.concatenate([linked, jnp.ones((TILE, DEG * TILE + G), jnp.bool_)], axis=1)
        scores = jnp.where(allowed[None], scores, -1e+30)
        highest = lax.optimization_barrier(jnp.max(scores, axis=2, keepdims=True))
        weights = jnp.exp(scores - highest)
        total_sum = lax.optimization_barrier(jnp.sum(weights, axis=2))
        rounded = lax.optimization_barrier(weights.astype(jnp.bfloat16)).astype(jnp.float32)
        blended = jnp.einsum('hqk,khd->qhd', rounded, value_rows.astype(jnp.float32), precision=lax.Precision.HIGHEST)
        blended = blended / jnp.transpose(total_sum)[..., None]
        return blended.astype(jnp.bfloat16).reshape(TILE, D)
    head_rows = lax.map(attend, jnp.arange(block_count, dtype=jnp.int32)).reshape(node_count, D)
    node_out = jnp.dot(head_rows, w_out, preferred_element_type=jnp.float32).astype(jnp.bfloat16)
    virtual_scores = jnp.einsum('ghd,nhd->hgn', virtual_queries.astype(jnp.float32), keys_all.reshape(node_count, H, head_size).astype(jnp.float32), precision=lax.Precision.HIGHEST) * score_scale
    highest = lax.optimization_barrier(jnp.max(virtual_scores, axis=2, keepdims=True))
    weights = jnp.exp(virtual_scores - highest)
    total_sum = lax.optimization_barrier(jnp.sum(weights, axis=2))
    weighted = jnp.einsum('hgn,nhd->hgd', weights, values_all.reshape(node_count, H, head_size).astype(jnp.float32), precision=lax.Precision.HIGHEST)
    virtual_heads = jnp.transpose(weighted / total_sum[..., None], (1, 0, 2)).reshape(G, D).astype(jnp.bfloat16)
    virtual_out = jnp.dot(virtual_heads, w_out, preferred_element_type=jnp.float32).astype(jnp.bfloat16)
    return (node_out, virtual_out)
```

```python
import functools
import math

import jax
import jax.numpy as jnp
from jax import lax
from jax.experimental import pallas as pl
from jax.experimental.pallas import tpu as pltpu
from jax.sharding import PartitionSpec as P

D = 256
H = 8
TILE = 128
G = 4


def project(source, weight):
    return jnp.dot(source, weight, preferred_element_type=jnp.float32).astype(jnp.bfloat16)


def shards(features, virtual_state, w_query, w_key, w_value, w_out, tile_map, local_nbr):
    row_count = features.shape[0]
    part_width = w_query.shape[1]
    head_size = D // H
    head_count = part_width // head_size
    score_scale = 1.0 / math.sqrt(head_size)
    block_count = row_count // TILE
    degree = tile_map.shape[1]
    peer_count = lax.axis_size("nodes")
    per_peer = block_count * degree // peer_count
    request_count = block_count * degree
    queries = project(features, w_query)
    keys_here = project(features, w_key)
    values_here = project(features, w_value)
    key_value = jnp.concatenate([keys_here, values_here], axis=1)
    flat_ids = tile_map.reshape(-1)
    owner_dev = flat_ids // block_count
    within = flat_ids % block_count
    owner_hits = (owner_dev[:, None] == jnp.arange(peer_count, dtype=jnp.int32)[None, :]).astype(
        jnp.int32
    )
    earlier_hits = jnp.cumsum(owner_hits, axis=0) - owner_hits
    position = jnp.sum(earlier_hits * owner_hits, axis=1)
    slot_of = owner_dev * per_peer + position
    placed = slot_of[:, None] == jnp.arange(request_count, dtype=jnp.int32)[None, :]
    ordered = jnp.sum(jnp.where(placed, within[:, None], 0), axis=0)
    wanted = lax.all_to_all(
        ordered.reshape(peer_count, per_peer), "nodes", split_axis=0, concat_axis=0, tiled=True
    ).reshape(-1)
    outgoing = key_value.reshape(block_count, TILE, 2 * part_width)[wanted]
    arrived = lax.all_to_all(outgoing, "nodes", split_axis=0, concat_axis=0, tiled=True)
    neighbour_tiles = arrived[slot_of]
    virtual_queries = project(virtual_state, w_query).reshape(G, head_count, head_size)
    virtual_keys = project(virtual_state, w_key)
    virtual_values = project(virtual_state, w_value)
    virtual_scores = (
        jnp.einsum(
            "ghd,nhd->hgn",
            virtual_queries,
            keys_here.reshape(row_count, head_count, head_size),
            preferred_element_type=jnp.float32,
        )
        * score_scale
    )
    values_wide = values_here.reshape(row_count, head_count, head_size).astype(jnp.float32)
    highest = lax.pmax(jnp.max(virtual_scores, axis=2), "nodes")
    weights = jnp.exp(virtual_scores - highest[..., None])
    total_part = jnp.sum(weights, axis=2)
    weighted_part = jnp.einsum(
        "hgn,nhd->hgd", weights, values_wide, precision=lax.Precision.HIGHEST
    )
    total_sum, weighted = lax.psum((total_part, weighted_part), "nodes")
    virtual_heads = (
        jnp.transpose(weighted / total_sum[..., None], (1, 0, 2))
        .reshape(G, part_width)
        .astype(jnp.bfloat16)
    )
    bundle = 4
    group_count = block_count // bundle
    virtual_pair = jnp.concatenate([virtual_keys, virtual_values], axis=1)
    columns = jnp.arange(TILE, dtype=jnp.int32)

    def attend(inputs_now):
        query_group, own_group, other_group, link_group = inputs_now
        virtual_rows = jnp.broadcast_to(virtual_pair[None], (bundle, G, 2 * part_width))
        gathered = jnp.concatenate([own_group, other_group, virtual_rows], axis=1)
        key_count = gathered.shape[1]
        key_part = gathered[:, :, :part_width].reshape(bundle, key_count, head_count, head_size)
        value_part = gathered[:, :, part_width:].reshape(bundle, key_count, head_count, head_size)
        scores = (
            jnp.einsum("bqhd,bkhd->bhqk", query_group, key_part, preferred_element_type=jnp.float32)
            * score_scale
        )
        linked = jnp.any(link_group[:, :, :, None] == columns[None, None, None, :], axis=2)
        allowed = jnp.concatenate(
            [linked, jnp.ones((bundle, TILE, key_count - TILE), jnp.bool_)], axis=2
        )
        scores = jnp.where(allowed[:, None], scores, -1e30)
        highest = jnp.max(scores, axis=3, keepdims=True)
        weights = jnp.exp(scores - highest)
        total_rows = jnp.sum(weights, axis=3)
        blended = jnp.einsum(
            "bhqk,bkhd->bqhd",
            weights.astype(jnp.bfloat16),
            value_part,
            preferred_element_type=jnp.float32,
        )
        blended = blended / jnp.transpose(total_rows, (0, 2, 1))[..., None]
        return blended.astype(jnp.bfloat16).reshape(bundle * TILE, part_width)

    head_rows = lax.map(
        attend,
        (
            queries.reshape(group_count, bundle, TILE, head_count, head_size),
            key_value.reshape(group_count, bundle, TILE, 2 * part_width),
            neighbour_tiles.reshape(group_count, bundle, degree * TILE, 2 * part_width),
            local_nbr.reshape(group_count, bundle, TILE, local_nbr.shape[1]),
        ),
    ).reshape(row_count, part_width)
    rows_whole, virtual_whole, weight_whole = (
        lax.all_gather(head_rows, "rep", axis=1, tiled=True),
        lax.all_gather(virtual_heads, "rep", axis=1, tiled=True),
        lax.all_gather(w_out, "rep", axis=0, tiled=True),
    )
    own_start = lax.axis_index("rep") * part_width
    weight_cols = lax.dynamic_slice_in_dim(weight_whole, own_start, part_width, 1)
    node_sum = jnp.dot(rows_whole, weight_cols, preferred_element_type=jnp.float32)
    virtual_sum = jnp.dot(virtual_whole, weight_cols, preferred_element_type=jnp.float32)
    return (node_sum.astype(jnp.bfloat16), virtual_sum.astype(jnp.bfloat16))


MESH = pl.DeviceIdType.MESH
LOG2E = 1.4426950408889634
VPAD = 16
UNIT = 64
NEG = -1e30


def nt(a, b):
    return lax.dot_general(a, b, (((1,), (1,)), ((), ())), preferred_element_type=jnp.float32)


def nn(a, b):
    return lax.dot_general(a, b, (((1,), (0,)), ((), ())), preferred_element_type=jnp.float32)


def tn(a, b):
    return lax.dot_general(a, b, (((0,), (0,)), ((), ())), preferred_element_type=jnp.float32)


def fused(
    peers, reps, side, middle,
    features, vstate, weights, tiles, links, out, vout,
    buf, wall, stage, vheads,
    own_sem, plane_recv, x_recv, core_recv, up_send, down_send, y_send, x_send, core_send,
    w_send, w_recv, o_send, o_recv, v_send, v_recv,
):
    units = features.shape[0]
    rows = units * UNIT
    half = units // 2
    width = features.shape[2] // reps
    head_size = D // H
    head_count = width // head_size
    coef = LOG2E / math.sqrt(head_size)
    blocks = rows // TILE // reps
    degree = tiles.shape[1]
    depth = peers // 2
    node, rep = lax.axis_index("nodes"), lax.axis_index("rep")
    z, y, x, core = node // 2, node % 2, rep // 2, rep % 2
    at_up, at_down = z < depth - 1, z > 0
    to_up, to_down = {"nodes": node + 2}, {"nodes": node - 2}
    to_y = {"nodes": z * 2 + (1 - y)}
    to_core, to_x, to_cross = (
        {"rep": x * 2 + (1 - core)},
        {"rep": (1 - x) * 2 + core},
        {"rep": (1 - x) * 2 + (1 - core)},
    )
    mates = (
        (to_core, x * 2 + (1 - core)),
        (to_x, (1 - x) * 2 + core),
        (to_cross, (1 - x) * 2 + (1 - core)),
    )

    own = pltpu.make_async_copy(features, buf.at[pl.ds(node * units, units)], own_sem.at[0])
    own.start()
    own_w = pltpu.make_async_copy(
        weights, wall.at[:, pl.ds(pl.multiple_of(rep * width, 16), width)], own_sem.at[1]
    )
    own_w.start()

    barrier = pltpu.get_barrier_semaphore()
    for target in (to_y, to_core, to_x, to_cross):
        pl.semaphore_signal(barrier, inc=1, device_id=target, device_id_type=MESH)

    @pl.when(at_up)
    def _():
        pl.semaphore_signal(barrier, inc=1, device_id=to_up, device_id_type=MESH)

    @pl.when(at_down)
    def _():
        pl.semaphore_signal(barrier, inc=1, device_id=to_down, device_id_type=MESH)

    pl.semaphore_wait(barrier, 4 + at_up.astype(jnp.int32) + at_down.astype(jnp.int32))

    pending = []

    def piece(chunk, which_core, kind):
        if kind == 0:
            start, size = x * (side + middle), side
        elif kind == 1:
            start, size = side, middle
        else:
            start, size = (1 - x) * (side + middle), side
        return buf.at[pl.ds(chunk * units + which_core * half + start, size)]

    def move(chunk, which_core, kind, send, recv, target):
        ref = piece(chunk, which_core, kind)
        return pltpu.make_async_remote_copy(
            src_ref=ref, dst_ref=ref, send_sem=send, recv_sem=recv, device_id=target, device_id_type=MESH
        )

    def issue(cond, make):
        if cond is None:
            make().start()
        else:
            @pl.when(cond)
            def _():
                make().start()
        pending.append((cond, make))

    def go_up(cond, chunk, kind):
        issue(cond, lambda: move(chunk, core, kind, up_send.at[chunk, kind], plane_recv.at[chunk, kind], to_up))

    def go_down(cond, chunk, kind):
        issue(cond, lambda: move(chunk, core, kind, down_send.at[chunk, kind], plane_recv.at[chunk, kind], to_down))

    def go_y(cond, chunk, kind):
        issue(cond, lambda: move(chunk, core, kind, y_send.at[chunk, kind], plane_recv.at[chunk, kind], to_y))

    def go_x(cond, chunk):
        issue(cond, lambda: move(chunk, core, 0, x_send.at[chunk], x_recv.at[chunk], to_x))

    def go_core(cond, chunk, kind):
        issue(cond, lambda: move(chunk, core, kind, core_send.at[chunk, kind], core_recv.at[chunk, kind], to_core))

    def wait_plane(cond, chunk, kind):
        def run():
            move(chunk, core, kind, y_send.at[chunk, kind], plane_recv.at[chunk, kind], to_y).wait_recv()

        if cond is None:
            run()
        else:
            pl.when(cond)(run)

    def wait_x(cond, chunk):
        def run():
            move(chunk, core, 2, x_send.at[chunk], x_recv.at[chunk], to_x).wait_recv()

        if cond is None:
            run()
        else:
            pl.when(cond)(run)

    own.wait()
    for kind in (0, 1):
        go_up(at_up, node, kind)
        go_down(at_down, node, kind)
        go_y(None, node, kind)
    own_w.wait()
    for index, (target, _) in enumerate(mates):
        wref = wall.at[:, pl.ds(pl.multiple_of(rep * width, 16), width)]
        issue(
            None,
            lambda wref=wref, index=index, target=target: pltpu.make_async_remote_copy(
                src_ref=wref, dst_ref=wref, send_sem=w_send.at[index], recv_sem=w_recv.at[rep],
                device_id=target, device_id_type=MESH,
            ),
        )

    def step_chunks(step, line):
        if step == 0:
            return [(None, z * 2 + line, None)]
        return [
            (z >= step, (z - step) * 2 + line, "up"),
            (z + step < depth, (z + step) * 2 + line, "down"),
        ]

    def x_arrivals(step):
        for line in (y, 1 - y):
            if step == 0 and line is y:
                continue
            for cond, chunk, _ in step_chunks(step, line):
                wait_x(cond, chunk)
                go_core(cond, chunk, 2)

    for step in range(1, depth + 1):
        for kind in (0, 1):
            if step < depth:
                for cond, chunk, way in step_chunks(step, y):
                    wait_plane(cond, chunk, kind)
                    if way == "up":
                        go_up(cond & at_up, chunk, kind)
                    else:
                        go_down(cond & at_down, chunk, kind)
                    go_y(cond, chunk, kind)
                    if kind == 0:
                        go_x(cond, chunk)
                    go_core(cond, chunk, kind)
            for cond, chunk, _ in step_chunks(step - 1, 1 - y):
                wait_plane(cond, chunk, kind)
                if kind == 0:
                    go_x(cond, chunk)
                go_core(cond, chunk, kind)
        if step >= 2:
            x_arrivals(step - 2)
    x_arrivals(depth - 1)

    for _, mate in mates:
        wref = wall.at[:, pl.ds(pl.multiple_of(mate * width, 16), width)]
        pltpu.make_async_remote_copy(
            src_ref=wref, dst_ref=wref, send_sem=w_send.at[0], recv_sem=w_recv.at[mate],
            device_id=to_core, device_id_type=MESH,
        ).wait_recv()
    for offset in range(1, peers):
        chunk = lax.rem(node + offset, peers)
        for kind in range(3):
            move(chunk, 1 - core, kind, core_send.at[chunk, kind], core_recv.at[chunk, kind], to_core).wait_recv()
    for cond, make in pending:
        def run(make=make):
            make().wait_send()

        if cond is None:
            run()
        else:
            pl.when(cond)(run)

    lane = lax.broadcasted_iota(jnp.int32, (VPAD, 2 * width), 1)
    sub = lax.broadcasted_iota(jnp.int32, (VPAD, 2 * width), 0)
    kv_weight = jnp.concatenate([weights[1], weights[2]], axis=0)
    virtual = vstate[...]
    vq = nt(virtual, jnp.concatenate([weights[0], weights[0]], axis=0)).astype(jnp.bfloat16).astype(jnp.float32)
    group = head_count * G
    vq_rows = jnp.zeros((VPAD, 2 * width), jnp.float32)
    for h in range(head_count):
        moved = pltpu.roll(vq, h * G, 0) if h else vq
        keep = (lane >= h * head_size) & (lane < (h + 1) * head_size) & (sub >= h * G) & (sub < (h + 1) * G)
        vq_rows = jnp.where(keep, moved, vq_rows)
    vq_rows = vq_rows.astype(jnp.bfloat16)

    def over(chunk, carry):
        top, total, acc = carry
        part = buf[pl.ds(chunk * units, units)].reshape(rows, D)
        kv = nt(part, kv_weight).astype(jnp.bfloat16)
        scores = nt(vq_rows, kv)
        new_top = jnp.maximum(top, jnp.max(scores, axis=1, keepdims=True))
        keep = jnp.exp2((top - new_top) * coef)
        w = jnp.exp2((scores - new_top) * coef)
        high = w.astype(jnp.bfloat16)
        low = (w - high.astype(jnp.float32)).astype(jnp.bfloat16)
        total = total * keep + jnp.sum(w, axis=1, keepdims=True)
        acc = acc * keep + nn(high, kv) + nn(low, kv)
        return new_top, total, acc

    top, total, acc = lax.fori_loop(
        0, peers, over,
        (
            jnp.full((VPAD, 1), NEG, jnp.float32),
            jnp.zeros((VPAD, 1), jnp.float32),
            jnp.zeros((VPAD, 2 * width), jnp.float32),
        ),
    )
    acc = acc / total
    merged = jnp.zeros((VPAD, 2 * width), jnp.float32)
    for h in range(head_count):
        moved = pltpu.roll(acc, VPAD - h * G, 0) if h else acc
        keep = (lane >= width + h * head_size) & (lane < width + (h + 1) * head_size) & (sub < G)
        merged = jnp.where(keep, moved, merged)
    vheads[rep] = merged.astype(jnp.bfloat16)
    v_pending = []
    for index, (target, mate) in enumerate(mates):
        copy = pltpu.make_async_remote_copy(
            src_ref=vheads.at[rep], dst_ref=vheads.at[rep], send_sem=v_send.at[index],
            recv_sem=v_recv.at[rep], device_id=target, device_id_type=MESH,
        )
        copy.start()
        v_pending.append(copy)

    wq, wk, wv, wo = wall[0], wall[1], wall[2], wall[3]
    vk = nt(virtual, wk).astype(jnp.bfloat16)
    vvt = nt(wv, virtual).astype(jnp.bfloat16)
    dim_lane = lax.broadcasted_iota(jnp.int32, (TILE, D), 1)
    key_row = lax.broadcasted_iota(jnp.int32, (TILE, TILE), 0)
    pad_row = lax.broadcasted_iota(jnp.int32, (VPAD, 2 * TILE), 0)

    def out_copy(b, index, target, mate, slot):
        place = pl.multiple_of(slot * blocks * TILE + b * TILE, 16)
        return pltpu.make_async_remote_copy(
            src_ref=stage.at[b, mate], dst_ref=out.at[pl.ds(place, TILE)], send_sem=o_send.at[b, index],
            recv_sem=o_recv.at[b, slot], device_id=target, device_id_type=MESH,
        )

    def attend(b, carry):
        block = rep * blocks + b
        share = TILE // UNIT
        base = node * units + block * share
        parts = [buf[base + i] for i in range(share)]
        mine = jnp.concatenate(parts, axis=0)
        for j in range(degree):
            start = tiles[block, j] * share
            parts += [buf[start + i] for i in range(share)]
        source = jnp.concatenate(parts, axis=0)
        q = nt(mine, wq).astype(jnp.bfloat16)
        k = nt(source, wk).astype(jnp.bfloat16)
        vt = nt(wv, source).astype(jnp.bfloat16)
        lk = links[:, pl.ds(pl.multiple_of(block * TILE, TILE), TILE)]
        linked = key_row == lk[0:1, :]
        for i in range(1, links.shape[0]):
            linked = linked | (key_row == lk[i : i + 1, :])
        bias = jnp.where(linked, 0.0, NEG)
        bias = jnp.concatenate([bias, bias], axis=1)
        made = []
        for pair in range(H // 2):
            first = pair * 2
            qs = []
            for h in (first, first + 1):
                keep = (dim_lane >= h * head_size) & (dim_lane < (h + 1) * head_size)
                qs.append(jnp.where(keep, q, jnp.zeros_like(q)))
            qs = jnp.concatenate(qs, axis=0)
            s = nt(k, qs)
            sv = jnp.where(pad_row < G, nt(vk, qs), NEG)
            local = s[:TILE] + bias
            far = s[TILE:]
            highest = jnp.maximum(
                jnp.maximum(jnp.max(local, axis=0, keepdims=True), jnp.max(far, axis=0, keepdims=True)),
                jnp.max(sv, axis=0, keepdims=True),
            )
            wl = jnp.exp2((local - highest) * coef)
            wf = jnp.exp2((far - highest) * coef)
            ws = jnp.exp2((sv - highest) * coef)
            sums = (
                jnp.sum(wl, axis=0, keepdims=True)
                + jnp.sum(wf, axis=0, keepdims=True)
                + jnp.sum(ws, axis=0, keepdims=True)
            )
            w = jnp.concatenate([wl.astype(jnp.bfloat16), wf.astype(jnp.bfloat16)], axis=0)
            span = slice(first * head_size, (first + 2) * head_size)
            blend = nn(vt[span], w) + nn(vvt[span], ws.astype(jnp.bfloat16))
            blend = blend / sums
            made.append(blend[:head_size, :TILE])
            made.append(blend[head_size:, TILE:])
        head_t = jnp.concatenate(made, axis=0).astype(jnp.bfloat16)
        result = tn(head_t, wo).astype(jnp.bfloat16)
        for d in range(reps):
            stage[b, d] = result[:, d * width : (d + 1) * width]
        out[pl.ds(pl.multiple_of(rep * blocks * TILE + b * TILE, 16), TILE), :] = stage[b, rep]
        for index, (target, mate) in enumerate(mates):
            out_copy(b, index, target, mate, rep).start()
        return carry

    lax.fori_loop(0, blocks, attend, 0)

    for _, mate in mates:
        pltpu.make_async_remote_copy(
            src_ref=vheads.at[mate], dst_ref=vheads.at[mate], send_sem=v_send.at[0],
            recv_sem=v_recv.at[mate], device_id=to_core, device_id_type=MESH,
        ).wait_recv()
    for copy in v_pending:
        copy.wait_send()
    vsum = jnp.zeros((VPAD, D), jnp.float32)
    for d in range(reps):
        vsum = vsum + nn(vheads[d][:, width:], wo[d * width : (d + 1) * width])
    pick = vsum[:G, :width]
    for d in range(1, reps):
        pick = jnp.where(rep == d, vsum[:G, d * width : (d + 1) * width], pick)
    vout[...] = pick.astype(jnp.bfloat16)

    def finish(b, carry):
        for index, (target, mate) in enumerate(mates):
            out_copy(b, index, target, mate, rep).wait_send()
            out_copy(b, index, target, mate, mate).wait_recv()
        return carry

    lax.fori_loop(0, blocks, finish, 0)


def gathered(peers, reps, features, virtual_state, w_query, w_key, w_value, w_out, tile_map, local_nbr):
    rows = features.shape[0]
    width = w_query.shape[1]
    half = rows // UNIT // 2
    side = half * 5 // 16
    middle = half - 2 * side
    weights = jnp.stack([w_query.T, w_key.T, w_value.T, w_out])
    vstate = jnp.pad(virtual_state, ((0, VPAD - G), (0, 0)))
    blocks = rows // TILE // reps
    dma = pltpu.SemaphoreType.DMA
    vmem = pl.BlockSpec(memory_space=pltpu.VMEM)
    return pl.pallas_call(
        functools.partial(fused, peers, reps, side, middle),
        out_shape=(
            jax.ShapeDtypeStruct((rows, width), jnp.bfloat16),
            jax.ShapeDtypeStruct((G, width), jnp.bfloat16),
        ),
        in_specs=[
            pl.BlockSpec(memory_space=pl.ANY), vmem, vmem, pl.BlockSpec(memory_space=pltpu.SMEM), vmem,
        ],
        out_specs=(vmem, vmem),
        scratch_shapes=[
            pltpu.VMEM((peers * rows // UNIT, UNIT, D), jnp.bfloat16),
            pltpu.VMEM((4, D, D), jnp.bfloat16),
            pltpu.VMEM((blocks, reps, TILE, width), jnp.bfloat16),
            pltpu.VMEM((reps, VPAD, 2 * width), jnp.bfloat16),
            dma((2,)), dma((peers, 2)), dma((peers,)), dma((peers, 3)),
            dma((peers, 2)), dma((peers, 2)), dma((peers, 2)), dma((peers,)), dma((peers, 3)),
            dma((3,)), dma((reps,)), dma((blocks, 3)), dma((blocks, reps)), dma((3,)), dma((reps,)),
        ],
        compiler_params=pltpu.CompilerParams(
            collective_id=0, has_side_effects=True, vmem_limit_bytes=48 * 1024 * 1024
        ),
        name="exphormer",
    )(features.reshape(rows // UNIT, UNIT, D), vstate, weights, tile_map, local_nbr.T)


def solution(mesh):
    peers, reps = mesh.shape["nodes"], mesh.shape["rep"]

    def local(features, *rest):
        fits = peers * features.size * 2 <= 16 * 1024 * 1024
        if fits and reps == 4 and peers % 2 == 0:
            return gathered(peers, reps, features, *rest)
        return shards(features, *rest)

    in_specs = (
        P("nodes", None),
        P(),
        P(None, "rep"),
        P(None, "rep"),
        P(None, "rep"),
        P("rep", None),
        P("nodes", None),
        P("nodes", None),
    )
    out_specs = (P("nodes", "rep"), P(None, "rep"))
    return jax.shard_map(local, mesh=mesh, in_specs=in_specs, out_specs=out_specs, check_vma=False)
```

```python
import functools
import math

import jax
import jax.numpy as jnp
from jax import lax
from jax.experimental import pallas as pl
from jax.experimental.pallas import tpu as pltpu
from jax.sharding import PartitionSpec as P

D = 256
H = 8
TILE = 128
G = 4


def project(source, weight):
    return jnp.dot(source, weight, preferred_element_type=jnp.float32).astype(jnp.bfloat16)


def shards(features, virtual_state, w_query, w_key, w_value, w_out, tile_map, local_nbr):
    row_count = features.shape[0]
    part_width = w_query.shape[1]
    head_size = D // H
    head_count = part_width // head_size
    score_scale = 1.0 / math.sqrt(head_size)
    block_count = row_count // TILE
    degree = tile_map.shape[1]
    peer_count = lax.axis_size("nodes")
    per_peer = block_count * degree // peer_count
    request_count = block_count * degree
    queries = project(features, w_query)
    keys_here = project(features, w_key)
    values_here = project(features, w_value)
    key_value = jnp.concatenate([keys_here, values_here], axis=1)
    flat_ids = tile_map.reshape(-1)
    owner_dev = flat_ids // block_count
    within = flat_ids % block_count
    owner_hits = (owner_dev[:, None] == jnp.arange(peer_count, dtype=jnp.int32)[None, :]).astype(
        jnp.int32
    )
    earlier_hits = jnp.cumsum(owner_hits, axis=0) - owner_hits
    position = jnp.sum(earlier_hits * owner_hits, axis=1)
    slot_of = owner_dev * per_peer + position
    placed = slot_of[:, None] == jnp.arange(request_count, dtype=jnp.int32)[None, :]
    ordered = jnp.sum(jnp.where(placed, within[:, None], 0), axis=0)
    wanted = lax.all_to_all(
        ordered.reshape(peer_count, per_peer), "nodes", split_axis=0, concat_axis=0, tiled=True
    ).reshape(-1)
    outgoing = key_value.reshape(block_count, TILE, 2 * part_width)[wanted]
    arrived = lax.all_to_all(outgoing, "nodes", split_axis=0, concat_axis=0, tiled=True)
    neighbour_tiles = arrived[slot_of]
    virtual_queries = project(virtual_state, w_query).reshape(G, head_count, head_size)
    virtual_keys = project(virtual_state, w_key)
    virtual_values = project(virtual_state, w_value)
    virtual_scores = (
        jnp.einsum(
            "ghd,nhd->hgn",
            virtual_queries,
            keys_here.reshape(row_count, head_count, head_size),
            preferred_element_type=jnp.float32,
        )
        * score_scale
    )
    values_wide = values_here.reshape(row_count, head_count, head_size).astype(jnp.float32)
    highest = lax.pmax(jnp.max(virtual_scores, axis=2), "nodes")
    weights = jnp.exp(virtual_scores - highest[..., None])
    total_part = jnp.sum(weights, axis=2)
    weighted_part = jnp.einsum(
        "hgn,nhd->hgd", weights, values_wide, precision=lax.Precision.HIGHEST
    )
    total_sum, weighted = lax.psum((total_part, weighted_part), "nodes")
    virtual_heads = (
        jnp.transpose(weighted / total_sum[..., None], (1, 0, 2))
        .reshape(G, part_width)
        .astype(jnp.bfloat16)
    )
    bundle = 4
    group_count = block_count // bundle
    virtual_pair = jnp.concatenate([virtual_keys, virtual_values], axis=1)
    columns = jnp.arange(TILE, dtype=jnp.int32)

    def attend(inputs_now):
        query_group, own_group, other_group, link_group = inputs_now
        virtual_rows = jnp.broadcast_to(virtual_pair[None], (bundle, G, 2 * part_width))
        gathered = jnp.concatenate([own_group, other_group, virtual_rows], axis=1)
        key_count = gathered.shape[1]
        key_part = gathered[:, :, :part_width].reshape(bundle, key_count, head_count, head_size)
        value_part = gathered[:, :, part_width:].reshape(bundle, key_count, head_count, head_size)
        scores = (
            jnp.einsum("bqhd,bkhd->bhqk", query_group, key_part, preferred_element_type=jnp.float32)
            * score_scale
        )
        linked = jnp.any(link_group[:, :, :, None] == columns[None, None, None, :], axis=2)
        allowed = jnp.concatenate(
            [linked, jnp.ones((bundle, TILE, key_count - TILE), jnp.bool_)], axis=2
        )
        scores = jnp.where(allowed[:, None], scores, -1e30)
        highest = jnp.max(scores, axis=3, keepdims=True)
        weights = jnp.exp(scores - highest)
        total_rows = jnp.sum(weights, axis=3)
        blended = jnp.einsum(
            "bhqk,bkhd->bqhd",
            weights.astype(jnp.bfloat16),
            value_part,
            preferred_element_type=jnp.float32,
        )
        blended = blended / jnp.transpose(total_rows, (0, 2, 1))[..., None]
        return blended.astype(jnp.bfloat16).reshape(bundle * TILE, part_width)

    head_rows = lax.map(
        attend,
        (
            queries.reshape(group_count, bundle, TILE, head_count, head_size),
            key_value.reshape(group_count, bundle, TILE, 2 * part_width),
            neighbour_tiles.reshape(group_count, bundle, degree * TILE, 2 * part_width),
            local_nbr.reshape(group_count, bundle, TILE, local_nbr.shape[1]),
        ),
    ).reshape(row_count, part_width)
    rows_whole, virtual_whole, weight_whole = (
        lax.all_gather(head_rows, "rep", axis=1, tiled=True),
        lax.all_gather(virtual_heads, "rep", axis=1, tiled=True),
        lax.all_gather(w_out, "rep", axis=0, tiled=True),
    )
    own_start = lax.axis_index("rep") * part_width
    weight_cols = lax.dynamic_slice_in_dim(weight_whole, own_start, part_width, 1)
    node_sum = jnp.dot(rows_whole, weight_cols, preferred_element_type=jnp.float32)
    virtual_sum = jnp.dot(virtual_whole, weight_cols, preferred_element_type=jnp.float32)
    return (node_sum.astype(jnp.bfloat16), virtual_sum.astype(jnp.bfloat16))


MESH = pl.DeviceIdType.MESH
LOG2E = 1.4426950408889634
VPAD = 16
UNIT = 32
NEG = -1e30


def nt(a, b):
    return lax.dot_general(a, b, (((1,), (1,)), ((), ())), preferred_element_type=jnp.float32)


def nn(a, b):
    return lax.dot_general(a, b, (((1,), (0,)), ((), ())), preferred_element_type=jnp.float32)


def tn(a, b):
    return lax.dot_general(a, b, (((0,), (0,)), ((), ())), preferred_element_type=jnp.float32)


def fused(
    peers, reps, near_side, far_side,
    features, vstate, weights, tiles, links, out, vout,
    buf, wall, stage, vheads, top_ref, total_ref, acc_ref,
    own_sem, plane_recv, x_recv, core_recv, up_send, down_send, y_send, x_send, core_send,
    w_send, w_recv, o_send, o_recv, v_send, v_recv,
):
    units = features.shape[0]
    rows = units * UNIT
    half = units // 2
    width = features.shape[2] // reps
    head_size = D // H
    head_count = width // head_size
    coef = LOG2E / math.sqrt(head_size)
    blocks = rows // TILE // reps
    degree = tiles.shape[1]
    depth = peers // 2
    node, rep = lax.axis_index("nodes"), lax.axis_index("rep")
    z, y, x, core = node // 2, node % 2, rep // 2, rep % 2
    at_up, at_down = z < depth - 1, z > 0
    to_up, to_down = {"nodes": node + 2}, {"nodes": node - 2}
    to_y = {"nodes": z * 2 + (1 - y)}
    to_core, to_x, to_cross = (
        {"rep": x * 2 + (1 - core)},
        {"rep": (1 - x) * 2 + core},
        {"rep": (1 - x) * 2 + (1 - core)},
    )
    mates = (
        (to_core, x * 2 + (1 - core)),
        (to_x, (1 - x) * 2 + core),
        (to_cross, (1 - x) * 2 + (1 - core)),
    )

    own = pltpu.make_async_copy(features, buf.at[pl.ds(node * units, units)], own_sem.at[0])
    own_w = pltpu.make_async_copy(
        weights, wall.at[:, pl.ds(pl.multiple_of(rep * width, 16), width)], own_sem.at[1]
    )
    own.start()
    own_w.start()

    barrier = pltpu.get_barrier_semaphore()
    for target in (to_y, to_core, to_x, to_cross):
        pl.semaphore_signal(barrier, inc=1, device_id=target, device_id_type=MESH)

    @pl.when(at_up)
    def _():
        pl.semaphore_signal(barrier, inc=1, device_id=to_up, device_id_type=MESH)

    @pl.when(at_down)
    def _():
        pl.semaphore_signal(barrier, inc=1, device_id=to_down, device_id_type=MESH)

    pl.semaphore_wait(barrier, 4 + at_up.astype(jnp.int32) + at_down.astype(jnp.int32))

    pending = []
    spans = {
        "first": (0, far_side),
        "rest": (far_side, half - near_side - far_side),
        "centre": (far_side, half - 2 * far_side),
        "edge": (0, near_side),
    }

    def begin(which_core, kind, plane):
        start, size = spans[kind]
        return which_core * half + start + plane * (half - 2 * start - size), size

    def piece(chunk, which_core, kind, plane=x):
        start, size = begin(which_core, kind, plane)
        return buf.at[pl.ds(chunk * units + start, size)]

    def move(chunk, which_core, kind, send, recv, target, plane=x):
        ref = piece(chunk, which_core, kind, plane)
        return pltpu.make_async_remote_copy(
            src_ref=ref, dst_ref=ref, send_sem=send, recv_sem=recv, device_id=target, device_id_type=MESH
        )

    def under(cond, run):
        if cond is None:
            run()
        else:
            pl.when(cond)(run)

    def issue(cond, make):
        under(cond, lambda: make().start())
        pending.append((cond, make))

    def push(cond, sems, chunk, slot, kind, target):
        issue(cond, lambda: move(chunk, core, kind, sems.at[chunk, slot], plane_recv.at[chunk, slot], target))

    def push_own(cond, sems, slot, kind, target):
        def make():
            start, size = begin(core, kind, x)
            return pltpu.make_async_remote_copy(
                src_ref=features.at[pl.ds(start, size)], dst_ref=piece(node, core, kind),
                send_sem=sems.at[node, slot], recv_sem=plane_recv.at[node, slot],
                device_id=target, device_id_type=MESH,
            )

        issue(cond, make)

    def go_x(cond, chunk, kind):
        issue(cond, lambda: move(chunk, core, kind, x_send.at[chunk], x_recv.at[chunk], to_x))

    def go_core(cond, chunk, slot, kind, plane=x):
        issue(
            cond,
            lambda: move(
                chunk, core, kind, core_send.at[chunk, slot], core_recv.at[chunk, slot], to_core, plane
            ),
        )

    def wait_plane(cond, chunk, slot, kind):
        under(
            cond,
            lambda: move(chunk, core, kind, y_send.at[chunk, slot], plane_recv.at[chunk, slot], to_y).wait_recv(),
        )

    for slot in (0, 1):
        push_own(at_up, up_send, slot, ("first", "rest")[slot], to_up)
        push_own(at_down, down_send, slot, ("first", "rest")[slot], to_down)
        push_own(None, y_send, slot, ("first", "centre")[slot], to_y)
    own_w.wait()
    for index, (target, _) in enumerate(mates):
        wref = wall.at[:, pl.ds(pl.multiple_of(rep * width, 16), width)]
        issue(
            None,
            lambda wref=wref, index=index, target=target: pltpu.make_async_remote_copy(
                src_ref=wref, dst_ref=wref, send_sem=w_send.at[index], recv_sem=w_recv.at[rep],
                device_id=target, device_id_type=MESH,
            ),
        )

    lane = lax.broadcasted_iota(jnp.int32, (VPAD, 2 * width), 1)
    sub = lax.broadcasted_iota(jnp.int32, (VPAD, 2 * width), 0)
    kv_weight = jnp.concatenate([weights[1], weights[2]], axis=0)
    virtual = vstate[...]
    vq = nt(virtual, jnp.concatenate([weights[0], weights[0]], axis=0)).astype(jnp.bfloat16).astype(jnp.float32)
    vq_rows = jnp.zeros((VPAD, 2 * width), jnp.float32)
    for h in range(head_count):
        moved = pltpu.roll(vq, h * G, 0) if h else vq
        keep = (lane >= h * head_size) & (lane < (h + 1) * head_size) & (sub >= h * G) & (sub < (h + 1) * G)
        vq_rows = jnp.where(keep, moved, vq_rows)
    vq_rows = vq_rows.astype(jnp.bfloat16)
    top_ref[...] = jnp.full((VPAD, 2 * width), NEG, jnp.float32)
    total_ref[...] = jnp.zeros((VPAD, 2 * width), jnp.float32)
    acc_ref[...] = jnp.zeros((VPAD, 2 * width), jnp.float32)

    def absorb(chunk):
        top = top_ref[:, :1]
        part = buf[pl.ds(chunk * units, units)].reshape(rows, D)
        kv = nt(part, kv_weight).astype(jnp.bfloat16)
        scores = nt(vq_rows, kv)
        new_top = jnp.maximum(top, jnp.max(scores, axis=1, keepdims=True))
        keep = jnp.exp2((top - new_top) * coef)
        w = jnp.exp2((scores - new_top) * coef)
        high = w.astype(jnp.bfloat16)
        low = (w - high.astype(jnp.float32)).astype(jnp.bfloat16)
        both = nn(jnp.concatenate([high, low], axis=0), kv)
        top_ref[...] = jnp.broadcast_to(new_top, (VPAD, 2 * width))
        total_ref[...] = total_ref[...] * keep + jnp.sum(w, axis=1, keepdims=True)
        acc_ref[...] = acc_ref[...] * keep + both[:VPAD] + both[VPAD:]

    own.wait()
    absorb(node)

    def step_chunks(step, line):
        if step == 0:
            return [(None, z * 2 + line, None)]
        return [
            (z >= step, (z - step) * 2 + line, "up"),
            (z + step < depth, (z + step) * 2 + line, "down"),
        ]

    def groups(step):
        if step > 0:
            for cond, chunk, _ in step_chunks(step, y):
                yield cond, chunk, ("first", "rest", "edge")
        for cond, chunk, _ in step_chunks(step, 1 - y):
            yield cond, chunk, ("first", "centre", "first")

    def x_arrivals(step):
        for cond, chunk, kinds in groups(step):
            under(
                cond,
                lambda: move(chunk, core, kinds[2], x_send.at[chunk], x_recv.at[chunk], to_x, 1 - x).wait_recv(),
            )
            go_core(cond, chunk, 2, kinds[2], 1 - x)

    def complete(step):
        for cond, chunk, kinds in groups(step):
            def run():
                for slot in range(3):
                    plane = 1 - x if slot == 2 else x
                    move(
                        chunk, 1 - core, kinds[slot], core_send.at[chunk, slot],
                        core_recv.at[chunk, slot], to_core, plane,
                    ).wait_recv()
                absorb(chunk)

            under(cond, run)

    for step in range(1, depth + 1):
        for slot in (0, 1):
            if step < depth:
                for cond, chunk, way in step_chunks(step, y):
                    kind = ("first", "rest")[slot]
                    wait_plane(cond, chunk, slot, kind)
                    if way == "up":
                        push(cond & at_up, up_send, chunk, slot, kind, to_up)
                    else:
                        push(cond & at_down, down_send, chunk, slot, kind, to_down)
                    push(cond, y_send, chunk, slot, ("first", "centre")[slot], to_y)
                    if slot == 0:
                        go_x(cond, chunk, "edge")
                    go_core(cond, chunk, slot, kind)
            for cond, chunk, _ in step_chunks(step - 1, 1 - y):
                kind = ("first", "centre")[slot]
                wait_plane(cond, chunk, slot, kind)
                if slot == 0:
                    go_x(cond, chunk, "first")
                go_core(cond, chunk, slot, kind)
        if step >= 2:
            x_arrivals(step - 2)
            complete(step - 2)
    x_arrivals(depth - 1)
    complete(depth - 1)

    for _, mate in mates:
        wref = wall.at[:, pl.ds(pl.multiple_of(mate * width, 16), width)]
        pltpu.make_async_remote_copy(
            src_ref=wref, dst_ref=wref, send_sem=w_send.at[0], recv_sem=w_recv.at[mate],
            device_id=to_core, device_id_type=MESH,
        ).wait_recv()

    acc, total = acc_ref[...], total_ref[...]
    acc = acc / total
    merged = jnp.zeros((VPAD, 2 * width), jnp.float32)
    for h in range(head_count):
        moved = pltpu.roll(acc, VPAD - h * G, 0) if h else acc
        keep = (lane >= width + h * head_size) & (lane < width + (h + 1) * head_size) & (sub < G)
        merged = jnp.where(keep, moved, merged)
    vheads[rep] = merged.astype(jnp.bfloat16)
    v_pending = []
    for index, (target, mate) in enumerate(mates):
        copy = pltpu.make_async_remote_copy(
            src_ref=vheads.at[rep], dst_ref=vheads.at[rep], send_sem=v_send.at[index],
            recv_sem=v_recv.at[rep], device_id=target, device_id_type=MESH,
        )
        copy.start()
        v_pending.append(copy)

    wq, wk, wv, wo = wall[0], wall[1], wall[2], wall[3]
    vk = nt(virtual, wk).astype(jnp.bfloat16)
    vvt = nt(wv, virtual).astype(jnp.bfloat16)
    dim_lane = lax.broadcasted_iota(jnp.int32, (TILE, D), 1)
    key_row = lax.broadcasted_iota(jnp.int32, (TILE, TILE), 0)
    pad_row = lax.broadcasted_iota(jnp.int32, (VPAD, 2 * TILE), 0)

    def out_copy(b, index, target, mate, slot):
        place = pl.multiple_of(slot * blocks * TILE + b * TILE, 16)
        return pltpu.make_async_remote_copy(
            src_ref=stage.at[b, mate], dst_ref=out.at[pl.ds(place, TILE)], send_sem=o_send.at[b, index],
            recv_sem=o_recv.at[b, slot], device_id=target, device_id_type=MESH,
        )

    def attend(b, carry):
        block = rep * blocks + b
        share = TILE // UNIT
        base = node * units + block * share
        parts = [buf[base + i] for i in range(share)]
        mine = jnp.concatenate(parts, axis=0)
        for j in range(degree):
            start = tiles[block, j] * share
            parts += [buf[start + i] for i in range(share)]
        source = jnp.concatenate(parts, axis=0)
        q = nt(mine, wq).astype(jnp.bfloat16)
        k = nt(source, wk).astype(jnp.bfloat16)
        vt = nt(wv, source).astype(jnp.bfloat16)
        lk = links[:, pl.ds(pl.multiple_of(block * TILE, TILE), TILE)]
        linked = key_row == lk[0:1, :]
        for i in range(1, links.shape[0]):
            linked = linked | (key_row == lk[i : i + 1, :])
        bias = jnp.where(linked, 0.0, NEG)
        bias = jnp.concatenate([bias, bias], axis=1)
        made = []
        for pair in range(H // 2):
            first = pair * 2
            qs = []
            for h in (first, first + 1):
                keep = (dim_lane >= h * head_size) & (dim_lane < (h + 1) * head_size)
                qs.append(jnp.where(keep, q, jnp.zeros_like(q)))
            qs = jnp.concatenate(qs, axis=0)
            s = nt(k, qs)
            sv = jnp.where(pad_row < G, nt(vk, qs), NEG)
            local = s[:TILE] + bias
            far = s[TILE:]
            highest = jnp.maximum(
                jnp.maximum(jnp.max(local, axis=0, keepdims=True), jnp.max(far, axis=0, keepdims=True)),
                jnp.max(sv, axis=0, keepdims=True),
            )
            wl = jnp.exp2((local - highest) * coef)
            wf = jnp.exp2((far - highest) * coef)
            ws = jnp.exp2((sv - highest) * coef)
            sums = (
                jnp.sum(wl, axis=0, keepdims=True)
                + jnp.sum(wf, axis=0, keepdims=True)
                + jnp.sum(ws, axis=0, keepdims=True)
            )
            w = jnp.concatenate([wl.astype(jnp.bfloat16), wf.astype(jnp.bfloat16)], axis=0)
            span = slice(first * head_size, (first + 2) * head_size)
            blend = nn(vt[span], w) + nn(vvt[span], ws.astype(jnp.bfloat16))
            blend = blend / sums
            made.append(blend[:head_size, :TILE])
            made.append(blend[head_size:, TILE:])
        head_t = jnp.concatenate(made, axis=0).astype(jnp.bfloat16)
        result = tn(head_t, wo).astype(jnp.bfloat16)
        for d in range(reps):
            stage[b, d] = result[:, d * width : (d + 1) * width]
        out[pl.ds(pl.multiple_of(rep * blocks * TILE + b * TILE, 16), TILE), :] = stage[b, rep]
        for index, (target, mate) in enumerate(mates):
            out_copy(b, index, target, mate, rep).start()
        return carry

    lax.fori_loop(0, blocks, attend, 0)

    for _, mate in mates:
        pltpu.make_async_remote_copy(
            src_ref=vheads.at[mate], dst_ref=vheads.at[mate], send_sem=v_send.at[0],
            recv_sem=v_recv.at[mate], device_id=to_core, device_id_type=MESH,
        ).wait_recv()
    for copy in v_pending:
        copy.wait_send()
    vsum = jnp.zeros((VPAD, D), jnp.float32)
    for d in range(reps):
        vsum = vsum + nn(vheads[d][:, width:], wo[d * width : (d + 1) * width])
    pick = vsum[:G, :width]
    for d in range(1, reps):
        pick = jnp.where(rep == d, vsum[:G, d * width : (d + 1) * width], pick)
    vout[...] = pick.astype(jnp.bfloat16)

    def finish(b, carry):
        for index, (target, mate) in enumerate(mates):
            out_copy(b, index, target, mate, rep).wait_send()
            out_copy(b, index, target, mate, mate).wait_recv()
        return carry

    lax.fori_loop(0, blocks, finish, 0)
    for cond, make in pending:
        under(cond, lambda: make().wait_send())


def gathered(peers, reps, features, virtual_state, w_query, w_key, w_value, w_out, tile_map, local_nbr):
    rows = features.shape[0]
    width = w_query.shape[1]
    half = rows // UNIT // 2
    near_side = half * 7 // 32
    far_side = half * 13 // 32
    weights = jnp.stack([w_query.T, w_key.T, w_value.T, w_out])
    vstate = jnp.pad(virtual_state, ((0, VPAD - G), (0, 0)))
    blocks = rows // TILE // reps
    dma = pltpu.SemaphoreType.DMA
    vmem = pl.BlockSpec(memory_space=pltpu.VMEM)
    return pl.pallas_call(
        functools.partial(fused, peers, reps, near_side, far_side),
        out_shape=(
            jax.ShapeDtypeStruct((rows, width), jnp.bfloat16),
            jax.ShapeDtypeStruct((G, width), jnp.bfloat16),
        ),
        in_specs=[
            pl.BlockSpec(memory_space=pl.ANY), vmem, vmem, pl.BlockSpec(memory_space=pltpu.SMEM), vmem,
        ],
        out_specs=(vmem, vmem),
        scratch_shapes=[
            pltpu.VMEM((peers * rows // UNIT, UNIT, D), jnp.bfloat16),
            pltpu.VMEM((4, D, D), jnp.bfloat16),
            pltpu.VMEM((blocks, reps, TILE, width), jnp.bfloat16),
            pltpu.VMEM((reps, VPAD, 2 * width), jnp.bfloat16),
            pltpu.VMEM((VPAD, 2 * width), jnp.float32),
            pltpu.VMEM((VPAD, 2 * width), jnp.float32),
            pltpu.VMEM((VPAD, 2 * width), jnp.float32),
            dma((2,)), dma((peers, 2)), dma((peers,)), dma((peers, 3)),
            dma((peers, 2)), dma((peers, 2)), dma((peers, 2)), dma((peers,)), dma((peers, 3)),
            dma((3,)), dma((reps,)), dma((blocks, 3)), dma((blocks, reps)), dma((3,)), dma((reps,)),
        ],
        compiler_params=pltpu.CompilerParams(
            collective_id=0, has_side_effects=True, vmem_limit_bytes=60 * 1024 * 1024
        ),
        name="exphormer",
    )(features.reshape(rows // UNIT, UNIT, D), vstate, weights, tile_map, local_nbr.T)


def solution(mesh):
    peers, reps = mesh.shape["nodes"], mesh.shape["rep"]

    def local(features, *rest):
        fits = peers * features.size * 2 <= 16 * 1024 * 1024
        if fits and reps == 4 and peers % 2 == 0:
            return gathered(peers, reps, features, *rest)
        return shards(features, *rest)

    in_specs = (
        P("nodes", None),
        P(),
        P(None, "rep"),
        P(None, "rep"),
        P(None, "rep"),
        P("rep", None),
        P("nodes", None),
        P("nodes", None),
    )
    out_specs = (P("nodes", "rep"), P(None, "rep"))
    return jax.shard_map(local, mesh=mesh, in_specs=in_specs, out_specs=out_specs, check_vma=False)
```

```python
import functools
import math

import jax
import jax.numpy as jnp
from jax import lax
from jax.experimental import pallas as pl
from jax.experimental.pallas import tpu as pltpu
from jax.sharding import PartitionSpec as P

D = 256
H = 8
TILE = 128
G = 4


def project(source, weight):
    return jnp.dot(source, weight, preferred_element_type=jnp.float32).astype(jnp.bfloat16)


def shards(features, virtual_state, w_query, w_key, w_value, w_out, tile_map, local_nbr):
    row_count = features.shape[0]
    part_width = w_query.shape[1]
    head_size = D // H
    head_count = part_width // head_size
    score_scale = 1.0 / math.sqrt(head_size)
    block_count = row_count // TILE
    degree = tile_map.shape[1]
    peer_count = lax.axis_size("nodes")
    per_peer = block_count * degree // peer_count
    request_count = block_count * degree
    queries = project(features, w_query)
    keys_here = project(features, w_key)
    values_here = project(features, w_value)
    key_value = jnp.concatenate([keys_here, values_here], axis=1)
    flat_ids = tile_map.reshape(-1)
    owner_dev = flat_ids // block_count
    within = flat_ids % block_count
    owner_hits = (owner_dev[:, None] == jnp.arange(peer_count, dtype=jnp.int32)[None, :]).astype(
        jnp.int32
    )
    earlier_hits = jnp.cumsum(owner_hits, axis=0) - owner_hits
    position = jnp.sum(earlier_hits * owner_hits, axis=1)
    slot_of = owner_dev * per_peer + position
    placed = slot_of[:, None] == jnp.arange(request_count, dtype=jnp.int32)[None, :]
    ordered = jnp.sum(jnp.where(placed, within[:, None], 0), axis=0)
    wanted = lax.all_to_all(
        ordered.reshape(peer_count, per_peer), "nodes", split_axis=0, concat_axis=0, tiled=True
    ).reshape(-1)
    outgoing = key_value.reshape(block_count, TILE, 2 * part_width)[wanted]
    arrived = lax.all_to_all(outgoing, "nodes", split_axis=0, concat_axis=0, tiled=True)
    neighbour_tiles = arrived[slot_of]
    virtual_queries = project(virtual_state, w_query).reshape(G, head_count, head_size)
    virtual_keys = project(virtual_state, w_key)
    virtual_values = project(virtual_state, w_value)
    virtual_scores = (
        jnp.einsum(
            "ghd,nhd->hgn",
            virtual_queries,
            keys_here.reshape(row_count, head_count, head_size),
            preferred_element_type=jnp.float32,
        )
        * score_scale
    )
    values_wide = values_here.reshape(row_count, head_count, head_size).astype(jnp.float32)
    highest = lax.pmax(jnp.max(virtual_scores, axis=2), "nodes")
    weights = jnp.exp(virtual_scores - highest[..., None])
    total_part = jnp.sum(weights, axis=2)
    weighted_part = jnp.einsum(
        "hgn,nhd->hgd", weights, values_wide, precision=lax.Precision.HIGHEST
    )
    total_sum, weighted = lax.psum((total_part, weighted_part), "nodes")
    virtual_heads = (
        jnp.transpose(weighted / total_sum[..., None], (1, 0, 2))
        .reshape(G, part_width)
        .astype(jnp.bfloat16)
    )
    bundle = 4
    group_count = block_count // bundle
    virtual_pair = jnp.concatenate([virtual_keys, virtual_values], axis=1)
    columns = jnp.arange(TILE, dtype=jnp.int32)

    def attend(inputs_now):
        query_group, own_group, other_group, link_group = inputs_now
        virtual_rows = jnp.broadcast_to(virtual_pair[None], (bundle, G, 2 * part_width))
        gathered = jnp.concatenate([own_group, other_group, virtual_rows], axis=1)
        key_count = gathered.shape[1]
        key_part = gathered[:, :, :part_width].reshape(bundle, key_count, head_count, head_size)
        value_part = gathered[:, :, part_width:].reshape(bundle, key_count, head_count, head_size)
        scores = (
            jnp.einsum("bqhd,bkhd->bhqk", query_group, key_part, preferred_element_type=jnp.float32)
            * score_scale
        )
        linked = jnp.any(link_group[:, :, :, None] == columns[None, None, None, :], axis=2)
        allowed = jnp.concatenate(
            [linked, jnp.ones((bundle, TILE, key_count - TILE), jnp.bool_)], axis=2
        )
        scores = jnp.where(allowed[:, None], scores, -1e30)
        highest = jnp.max(scores, axis=3, keepdims=True)
        weights = jnp.exp(scores - highest)
        total_rows = jnp.sum(weights, axis=3)
        blended = jnp.einsum(
            "bhqk,bkhd->bqhd",
            weights.astype(jnp.bfloat16),
            value_part,
            preferred_element_type=jnp.float32,
        )
        blended = blended / jnp.transpose(total_rows, (0, 2, 1))[..., None]
        return blended.astype(jnp.bfloat16).reshape(bundle * TILE, part_width)

    head_rows = lax.map(
        attend,
        (
            queries.reshape(group_count, bundle, TILE, head_count, head_size),
            key_value.reshape(group_count, bundle, TILE, 2 * part_width),
            neighbour_tiles.reshape(group_count, bundle, degree * TILE, 2 * part_width),
            local_nbr.reshape(group_count, bundle, TILE, local_nbr.shape[1]),
        ),
    ).reshape(row_count, part_width)
    rows_whole, virtual_whole, weight_whole = (
        lax.all_gather(head_rows, "rep", axis=1, tiled=True),
        lax.all_gather(virtual_heads, "rep", axis=1, tiled=True),
        lax.all_gather(w_out, "rep", axis=0, tiled=True),
    )
    own_start = lax.axis_index("rep") * part_width
    weight_cols = lax.dynamic_slice_in_dim(weight_whole, own_start, part_width, 1)
    node_sum = jnp.dot(rows_whole, weight_cols, preferred_element_type=jnp.float32)
    virtual_sum = jnp.dot(virtual_whole, weight_cols, preferred_element_type=jnp.float32)
    return (node_sum.astype(jnp.bfloat16), virtual_sum.astype(jnp.bfloat16))


MESH = pl.DeviceIdType.MESH
LOG2E = 1.4426950408889634
VPAD = 16
UNIT = 32
NEG = -1e30


def nt(a, b):
    return lax.dot_general(a, b, (((1,), (1,)), ((), ())), preferred_element_type=jnp.float32)


def nn(a, b):
    return lax.dot_general(a, b, (((1,), (0,)), ((), ())), preferred_element_type=jnp.float32)


def tn(a, b):
    return lax.dot_general(a, b, (((0,), (0,)), ((), ())), preferred_element_type=jnp.float32)


def fused(
    peers, reps, near_side, far_side,
    features, vstate, weights, tiles, links_in, out, vout,
    buf, wall, stage, vheads, links, vpad, top_ref, total_ref, acc_ref,
    own_sem, plane_recv, x_recv, core_recv, up_send, down_send, y_send, x_send, core_send,
    w_send, w_recv, o_send, o_recv, v_send, v_recv,
):
    units = features.shape[0]
    rows = units * UNIT
    half = units // 2
    width = features.shape[2] // reps
    head_size = D // H
    head_count = width // head_size
    coef = LOG2E / math.sqrt(head_size)
    blocks = rows // TILE // reps
    degree = tiles.shape[1]
    depth = peers // 2
    node, rep = lax.axis_index("nodes"), lax.axis_index("rep")
    z, y, x, core = node // 2, node % 2, rep // 2, rep % 2
    at_up, at_down = z < depth - 1, z > 0
    to_up, to_down = {"nodes": node + 2}, {"nodes": node - 2}
    to_y = {"nodes": z * 2 + (1 - y)}
    to_core, to_x, to_cross = (
        {"rep": x * 2 + (1 - core)},
        {"rep": (1 - x) * 2 + core},
        {"rep": (1 - x) * 2 + (1 - core)},
    )
    mates = (
        (to_core, x * 2 + (1 - core)),
        (to_x, (1 - x) * 2 + core),
        (to_cross, (1 - x) * 2 + (1 - core)),
    )

    own = pltpu.make_async_copy(features, buf.at[pl.ds(node * units, units)], own_sem.at[0])
    own_w = pltpu.make_async_copy(
        weights, wall.at[:, pl.ds(pl.multiple_of(rep * width, 16), width)], own_sem.at[1]
    )
    own_l = pltpu.make_async_copy(links_in, links, own_sem.at[2])
    own.start()
    own_w.start()
    own_l.start()

    barrier = pltpu.get_barrier_semaphore()
    for target in (to_y, to_core, to_x, to_cross):
        pl.semaphore_signal(barrier, inc=1, device_id=target, device_id_type=MESH)

    @pl.when(at_up)
    def _():
        pl.semaphore_signal(barrier, inc=1, device_id=to_up, device_id_type=MESH)

    @pl.when(at_down)
    def _():
        pl.semaphore_signal(barrier, inc=1, device_id=to_down, device_id_type=MESH)

    pl.semaphore_wait(barrier, 4 + at_up.astype(jnp.int32) + at_down.astype(jnp.int32))

    pending = []
    near_kinds, far_kinds = ("edge", "inner", "rest"), ("edge", "inner", "centre")
    slots = range(len(near_kinds))
    spans = {
        "edge": (0, near_side),
        "inner": (near_side, far_side - near_side),
        "rest": (far_side, half - near_side - far_side),
        "centre": (far_side, half - 2 * far_side),
    }

    def begin(which_core, kind, plane):
        start, size = spans[kind]
        return which_core * half + start + plane * (half - 2 * start - size), size

    def piece(chunk, which_core, kind, plane=x):
        start, size = begin(which_core, kind, plane)
        return buf.at[pl.ds(chunk * units + start, size)]

    def move(chunk, which_core, kind, send, recv, target, plane=x):
        ref = piece(chunk, which_core, kind, plane)
        return pltpu.make_async_remote_copy(
            src_ref=ref, dst_ref=ref, send_sem=send, recv_sem=recv, device_id=target, device_id_type=MESH
        )

    def under(cond, run):
        if cond is None:
            run()
        else:
            pl.when(cond)(run)

    def issue(cond, make):
        under(cond, lambda: make().start())
        pending.append((cond, make))

    def push(cond, sems, chunk, slot, kind, target):
        issue(cond, lambda: move(chunk, core, kind, sems.at[chunk, slot], plane_recv.at[chunk, slot], target))

    def push_own(cond, sems, slot, kind, target):
        def make():
            start, size = begin(core, kind, x)
            return pltpu.make_async_remote_copy(
                src_ref=features.at[pl.ds(start, size)], dst_ref=piece(node, core, kind),
                send_sem=sems.at[node, slot], recv_sem=plane_recv.at[node, slot],
                device_id=target, device_id_type=MESH,
            )

        issue(cond, make)

    def go_x(cond, chunk, slot):
        kind = near_kinds[slot]
        issue(cond, lambda: move(chunk, core, kind, x_send.at[chunk, slot], x_recv.at[chunk, slot], to_x))

    def go_core(cond, chunk, slot, kind, plane=x):
        issue(
            cond,
            lambda: move(
                chunk, core, kind, core_send.at[chunk, slot], core_recv.at[chunk, slot], to_core, plane
            ),
        )

    def wait_plane(cond, chunk, slot, kind):
        under(
            cond,
            lambda: move(chunk, core, kind, y_send.at[chunk, slot], plane_recv.at[chunk, slot], to_y).wait_recv(),
        )

    for slot in slots:
        push_own(at_up, up_send, slot, near_kinds[slot], to_up)
        push_own(at_down, down_send, slot, near_kinds[slot], to_down)
        push_own(None, y_send, slot, far_kinds[slot], to_y)
    own_w.wait()
    for index, (target, _) in enumerate(mates):
        wref = wall.at[:, pl.ds(pl.multiple_of(rep * width, 16), width)]
        issue(
            None,
            lambda wref=wref, index=index, target=target: pltpu.make_async_remote_copy(
                src_ref=wref, dst_ref=wref, send_sem=w_send.at[index], recv_sem=w_recv.at[rep],
                device_id=target, device_id_type=MESH,
            ),
        )

    lane = lax.broadcasted_iota(jnp.int32, (VPAD, 2 * width), 1)
    sub = lax.broadcasted_iota(jnp.int32, (VPAD, 2 * width), 0)
    kv_weight = jnp.concatenate([weights[1], weights[2]], axis=0)
    vpad[...] = jnp.zeros_like(vpad)
    vpad[:G] = vstate[...]
    virtual = vpad[...]
    vq = nt(virtual, jnp.concatenate([weights[0], weights[0]], axis=0)).astype(jnp.bfloat16).astype(jnp.float32)
    vq_rows = jnp.zeros((VPAD, 2 * width), jnp.float32)
    for h in range(head_count):
        moved = pltpu.roll(vq, h * G, 0) if h else vq
        keep = (lane >= h * head_size) & (lane < (h + 1) * head_size) & (sub >= h * G) & (sub < (h + 1) * G)
        vq_rows = jnp.where(keep, moved, vq_rows)
    vq_rows = vq_rows.astype(jnp.bfloat16)
    top_ref[...] = jnp.full((VPAD, 2 * width), NEG, jnp.float32)
    total_ref[...] = jnp.zeros((VPAD, 2 * width), jnp.float32)
    acc_ref[...] = jnp.zeros((VPAD, 2 * width), jnp.float32)

    def absorb(chunk):
        top = top_ref[:, :1]
        part = buf[pl.ds(chunk * units, units)].reshape(rows, D)
        kv = nt(part, kv_weight).astype(jnp.bfloat16)
        scores = nt(vq_rows, kv)
        new_top = jnp.maximum(top, jnp.max(scores, axis=1, keepdims=True))
        keep = jnp.exp2((top - new_top) * coef)
        w = jnp.exp2((scores - new_top) * coef)
        high = w.astype(jnp.bfloat16)
        low = (w - high.astype(jnp.float32)).astype(jnp.bfloat16)
        both = nn(jnp.concatenate([high, low], axis=0), kv)
        top_ref[...] = jnp.broadcast_to(new_top, (VPAD, 2 * width))
        total_ref[...] = total_ref[...] * keep + jnp.sum(w, axis=1, keepdims=True)
        acc_ref[...] = acc_ref[...] * keep + both[:VPAD] + both[VPAD:]

    own.wait()
    own_l.wait()
    absorb(node)

    def step_chunks(step, line):
        if step == 0:
            return [(None, z * 2 + line, None)]
        return [
            (z >= step, (z - step) * 2 + line, "up"),
            (z + step < depth, (z + step) * 2 + line, "down"),
        ]

    def groups(step):
        if step > 0:
            for cond, chunk, _ in step_chunks(step, y):
                yield cond, chunk, near_kinds, 1
        for cond, chunk, _ in step_chunks(step, 1 - y):
            yield cond, chunk, far_kinds, 2

    def x_arrivals(step):
        for slot in (0, 1):
            for cond, chunk, kinds, crossing in groups(step):
                if slot < crossing:
                    under(
                        cond,
                        lambda: move(
                            chunk, core, kinds[slot], x_send.at[chunk, slot], x_recv.at[chunk, slot], to_x, 1 - x
                        ).wait_recv(),
                    )
                    go_core(cond, chunk, len(slots) + slot, kinds[slot], 1 - x)

    def complete(step):
        for cond, chunk, kinds, crossing in groups(step):
            def run():
                for slot in range(len(slots) + crossing):
                    across = slot >= len(slots)
                    move(
                        chunk, 1 - core, kinds[slot - len(slots) if across else slot],
                        core_send.at[chunk, slot], core_recv.at[chunk, slot], to_core,
                        1 - x if across else x,
                    ).wait_recv()

            under(cond, run)

        def visit(i, carry):
            line, way = i % 2, i // 2
            place = z + (1 - 2 * way) * step
            fits = (place >= 0) & (place < depth)
            if step == 0:
                fits = i == 1 - y

            @pl.when(fits)
            def _():
                absorb(place * 2 + line)

            return carry

        lax.fori_loop(0, 2 if step == 0 else 4, visit, 0)

    for step in range(1, depth + 1):
        for slot in slots:
            if step < depth:
                for cond, chunk, way in step_chunks(step, y):
                    wait_plane(cond, chunk, slot, near_kinds[slot])
                    if way == "up":
                        push(cond & at_up, up_send, chunk, slot, near_kinds[slot], to_up)
                    else:
                        push(cond & at_down, down_send, chunk, slot, near_kinds[slot], to_down)
                    push(cond, y_send, chunk, slot, far_kinds[slot], to_y)
                    if slot == 0:
                        go_x(cond, chunk, slot)
                    go_core(cond, chunk, slot, near_kinds[slot])
            for cond, chunk, _ in step_chunks(step - 1, 1 - y):
                wait_plane(cond, chunk, slot, far_kinds[slot])
                if slot < 2:
                    go_x(cond, chunk, slot)
                go_core(cond, chunk, slot, far_kinds[slot])
        if step >= 2:
            x_arrivals(step - 2)
            complete(step - 2)
    x_arrivals(depth - 1)
    complete(depth - 1)

    for _, mate in mates:
        wref = wall.at[:, pl.ds(pl.multiple_of(mate * width, 16), width)]
        pltpu.make_async_remote_copy(
            src_ref=wref, dst_ref=wref, send_sem=w_send.at[0], recv_sem=w_recv.at[mate],
            device_id=to_core, device_id_type=MESH,
        ).wait_recv()

    acc, total = acc_ref[...], total_ref[...]
    acc = acc / total
    merged = jnp.zeros((VPAD, 2 * width), jnp.float32)
    for h in range(head_count):
        moved = pltpu.roll(acc, VPAD - h * G, 0) if h else acc
        keep = (lane >= width + h * head_size) & (lane < width + (h + 1) * head_size) & (sub < G)
        merged = jnp.where(keep, moved, merged)
    vheads[rep] = merged.astype(jnp.bfloat16)
    v_pending = []
    for index, (target, mate) in enumerate(mates):
        copy = pltpu.make_async_remote_copy(
            src_ref=vheads.at[rep], dst_ref=vheads.at[rep], send_sem=v_send.at[index],
            recv_sem=v_recv.at[rep], device_id=target, device_id_type=MESH,
        )
        copy.start()
        v_pending.append(copy)

    wq, wk, wv, wo = wall[0], wall[1], wall[2], wall[3]
    vk = nt(virtual, wk).astype(jnp.bfloat16)
    vvt = nt(wv, virtual).astype(jnp.bfloat16)
    dim_lane = lax.broadcasted_iota(jnp.int32, (TILE, D), 1)
    key_row = lax.broadcasted_iota(jnp.int32, (TILE, TILE), 0)
    pad_row = lax.broadcasted_iota(jnp.int32, (VPAD, 2 * TILE), 0)

    def out_copy(b, index, target, mate, slot):
        place = pl.multiple_of(slot * blocks * TILE + b * TILE, 16)
        return pltpu.make_async_remote_copy(
            src_ref=stage.at[b, mate], dst_ref=out.at[pl.ds(place, TILE)], send_sem=o_send.at[b, index],
            recv_sem=o_recv.at[b, slot], device_id=target, device_id_type=MESH,
        )

    def attend(b, carry):
        block = rep * blocks + b
        share = TILE // UNIT
        base = node * units + block * share
        parts = [buf[base + i] for i in range(share)]
        mine = jnp.concatenate(parts, axis=0)
        for j in range(degree):
            start = tiles[block, j] * share
            parts += [buf[start + i] for i in range(share)]
        source = jnp.concatenate(parts, axis=0)
        q = nt(mine, wq).astype(jnp.bfloat16)
        k = nt(source, wk).astype(jnp.bfloat16)
        vt = nt(wv, source).astype(jnp.bfloat16)
        lk = links[:, pl.ds(pl.multiple_of(block * TILE, TILE), TILE)]
        linked = key_row == lk[0:1, :]
        for i in range(1, links.shape[0]):
            linked = linked | (key_row == lk[i : i + 1, :])
        bias = jnp.where(linked, 0.0, NEG)
        bias = jnp.concatenate([bias, bias], axis=1)
        made = []
        for pair in range(H // 2):
            first = pair * 2
            qs = []
            for h in (first, first + 1):
                keep = (dim_lane >= h * head_size) & (dim_lane < (h + 1) * head_size)
                qs.append(jnp.where(keep, q, jnp.zeros_like(q)))
            qs = jnp.concatenate(qs, axis=0)
            s = nt(k, qs)
            sv = jnp.where(pad_row < G, nt(vk, qs), NEG)
            local = s[:TILE] + bias
            far = s[TILE:]
            highest = jnp.maximum(
                jnp.maximum(jnp.max(local, axis=0, keepdims=True), jnp.max(far, axis=0, keepdims=True)),
                jnp.max(sv, axis=0, keepdims=True),
            )
            wl = jnp.exp2((local - highest) * coef)
            wf = jnp.exp2((far - highest) * coef)
            ws = jnp.exp2((sv - highest) * coef)
            sums = (
                jnp.sum(wl, axis=0, keepdims=True)
                + jnp.sum(wf, axis=0, keepdims=True)
                + jnp.sum(ws, axis=0, keepdims=True)
            )
            w = jnp.concatenate([wl.astype(jnp.bfloat16), wf.astype(jnp.bfloat16)], axis=0)
            span = slice(first * head_size, (first + 2) * head_size)
            blend = nn(vt[span], w) + nn(vvt[span], ws.astype(jnp.bfloat16))
            blend = blend / sums
            made.append(blend[:head_size, :TILE])
            made.append(blend[head_size:, TILE:])
        head_t = jnp.concatenate(made, axis=0).astype(jnp.bfloat16)
        result = tn(head_t, wo).astype(jnp.bfloat16)
        for d in range(reps):
            stage[b, d] = result[:, d * width : (d + 1) * width]
        out[pl.ds(pl.multiple_of(rep * blocks * TILE + b * TILE, 16), TILE), :] = stage[b, rep]
        for index, (target, mate) in enumerate(mates):
            out_copy(b, index, target, mate, rep).start()
        return carry

    lax.fori_loop(0, blocks, attend, 0)

    for _, mate in mates:
        pltpu.make_async_remote_copy(
            src_ref=vheads.at[mate], dst_ref=vheads.at[mate], send_sem=v_send.at[0],
            recv_sem=v_recv.at[mate], device_id=to_core, device_id_type=MESH,
        ).wait_recv()
    for copy in v_pending:
        copy.wait_send()
    vsum = jnp.zeros((VPAD, D), jnp.float32)
    for d in range(reps):
        vsum = vsum + nn(vheads[d][:, width:], wo[d * width : (d + 1) * width])
    pick = vsum[:G, :width]
    for d in range(1, reps):
        pick = jnp.where(rep == d, vsum[:G, d * width : (d + 1) * width], pick)
    vout[...] = pick.astype(jnp.bfloat16)

    def finish(b, carry):
        for index, (target, mate) in enumerate(mates):
            out_copy(b, index, target, mate, rep).wait_send()
            out_copy(b, index, target, mate, mate).wait_recv()
        return carry

    lax.fori_loop(0, blocks, finish, 0)
    for cond, make in pending:
        under(cond, lambda: make().wait_send())


def gathered(peers, reps, features, virtual_state, w_query, w_key, w_value, w_out, tile_map, local_nbr):
    rows = features.shape[0]
    width = w_query.shape[1]
    half = rows // UNIT // 2
    near_side = half * 10 // 32
    far_side = half * 11 // 32
    weights = jnp.stack([w_query.T, w_key.T, w_value.T, w_out])
    blocks = rows // TILE // reps
    dma = pltpu.SemaphoreType.DMA
    vmem = pl.BlockSpec(memory_space=pltpu.VMEM)
    return pl.pallas_call(
        functools.partial(fused, peers, reps, near_side, far_side),
        out_shape=(
            jax.ShapeDtypeStruct((rows, width), jnp.bfloat16),
            jax.ShapeDtypeStruct((G, width), jnp.bfloat16),
        ),
        in_specs=[
            pl.BlockSpec(memory_space=pl.ANY), vmem, vmem,
            pl.BlockSpec(memory_space=pltpu.SMEM), pl.BlockSpec(memory_space=pl.ANY),
        ],
        out_specs=(vmem, vmem),
        scratch_shapes=[
            pltpu.VMEM((peers * rows // UNIT, UNIT, D), jnp.bfloat16),
            pltpu.VMEM((4, D, D), jnp.bfloat16),
            pltpu.VMEM((blocks, reps, TILE, width), jnp.bfloat16),
            pltpu.VMEM((reps, VPAD, 2 * width), jnp.bfloat16),
            pltpu.VMEM(local_nbr.shape[::-1], jnp.int32),
            pltpu.VMEM((VPAD, D), jnp.bfloat16),
            pltpu.VMEM((VPAD, 2 * width), jnp.float32),
            pltpu.VMEM((VPAD, 2 * width), jnp.float32),
            pltpu.VMEM((VPAD, 2 * width), jnp.float32),
            dma((3,)), dma((peers, 3)), dma((peers, 2)), dma((peers, 5)),
            dma((peers, 3)), dma((peers, 3)), dma((peers, 3)), dma((peers, 2)), dma((peers, 5)),
            dma((3,)), dma((reps,)), dma((blocks, 3)), dma((blocks, reps)), dma((3,)), dma((reps,)),
        ],
        compiler_params=pltpu.CompilerParams(
            collective_id=0, has_side_effects=True, vmem_limit_bytes=48 * 1024 * 1024
        ),
        name="exphormer",
    )(features.reshape(rows // UNIT, UNIT, D), virtual_state, weights, tile_map, local_nbr.T)


def solution(mesh):
    peers, reps = mesh.shape["nodes"], mesh.shape["rep"]

    def local(features, *rest):
        fits = peers * features.size * 2 <= 16 * 1024 * 1024
        if fits and reps == 4 and peers % 2 == 0:
            return gathered(peers, reps, features, *rest)
        return shards(features, *rest)

    in_specs = (
        P("nodes", None),
        P(),
        P(None, "rep"),
        P(None, "rep"),
        P(None, "rep"),
        P("rep", None),
        P("nodes", None),
        P("nodes", None),
    )
    out_specs = (P("nodes", "rep"), P(None, "rep"))
    return jax.shard_map(local, mesh=mesh, in_specs=in_specs, out_specs=out_specs, check_vma=False)
```

```python
import functools
import math

import jax
import jax.numpy as jnp
from jax import lax
from jax.experimental import pallas as pl
from jax.experimental.pallas import tpu as pltpu
from jax.sharding import PartitionSpec as P

D = 256
H = 8
TILE = 128
G = 4


def project(source, weight):
    return jnp.dot(source, weight, preferred_element_type=jnp.float32).astype(jnp.bfloat16)


def shards(features, virtual_state, w_query, w_key, w_value, w_out, tile_map, local_nbr):
    row_count = features.shape[0]
    part_width = w_query.shape[1]
    head_size = D // H
    head_count = part_width // head_size
    score_scale = 1.0 / math.sqrt(head_size)
    block_count = row_count // TILE
    degree = tile_map.shape[1]
    peer_count = lax.axis_size("nodes")
    per_peer = block_count * degree // peer_count
    request_count = block_count * degree
    queries = project(features, w_query)
    keys_here = project(features, w_key)
    values_here = project(features, w_value)
    key_value = jnp.concatenate([keys_here, values_here], axis=1)
    flat_ids = tile_map.reshape(-1)
    owner_dev = flat_ids // block_count
    within = flat_ids % block_count
    owner_hits = (owner_dev[:, None] == jnp.arange(peer_count, dtype=jnp.int32)[None, :]).astype(
        jnp.int32
    )
    earlier_hits = jnp.cumsum(owner_hits, axis=0) - owner_hits
    position = jnp.sum(earlier_hits * owner_hits, axis=1)
    slot_of = owner_dev * per_peer + position
    placed = slot_of[:, None] == jnp.arange(request_count, dtype=jnp.int32)[None, :]
    ordered = jnp.sum(jnp.where(placed, within[:, None], 0), axis=0)
    wanted = lax.all_to_all(
        ordered.reshape(peer_count, per_peer), "nodes", split_axis=0, concat_axis=0, tiled=True
    ).reshape(-1)
    outgoing = key_value.reshape(block_count, TILE, 2 * part_width)[wanted]
    arrived = lax.all_to_all(outgoing, "nodes", split_axis=0, concat_axis=0, tiled=True)
    neighbour_tiles = arrived[slot_of]
    virtual_queries = project(virtual_state, w_query).reshape(G, head_count, head_size)
    virtual_keys = project(virtual_state, w_key)
    virtual_values = project(virtual_state, w_value)
    virtual_scores = (
        jnp.einsum(
            "ghd,nhd->hgn",
            virtual_queries,
            keys_here.reshape(row_count, head_count, head_size),
            preferred_element_type=jnp.float32,
        )
        * score_scale
    )
    values_wide = values_here.reshape(row_count, head_count, head_size).astype(jnp.float32)
    highest = lax.pmax(jnp.max(virtual_scores, axis=2), "nodes")
    weights = jnp.exp(virtual_scores - highest[..., None])
    total_part = jnp.sum(weights, axis=2)
    weighted_part = jnp.einsum(
        "hgn,nhd->hgd", weights, values_wide, precision=lax.Precision.HIGHEST
    )
    total_sum, weighted = lax.psum((total_part, weighted_part), "nodes")
    virtual_heads = (
        jnp.transpose(weighted / total_sum[..., None], (1, 0, 2))
        .reshape(G, part_width)
        .astype(jnp.bfloat16)
    )
    bundle = 4
    group_count = block_count // bundle
    virtual_pair = jnp.concatenate([virtual_keys, virtual_values], axis=1)
    columns = jnp.arange(TILE, dtype=jnp.int32)

    def attend(inputs_now):
        query_group, own_group, other_group, link_group = inputs_now
        virtual_rows = jnp.broadcast_to(virtual_pair[None], (bundle, G, 2 * part_width))
        gathered = jnp.concatenate([own_group, other_group, virtual_rows], axis=1)
        key_count = gathered.shape[1]
        key_part = gathered[:, :, :part_width].reshape(bundle, key_count, head_count, head_size)
        value_part = gathered[:, :, part_width:].reshape(bundle, key_count, head_count, head_size)
        scores = (
            jnp.einsum("bqhd,bkhd->bhqk", query_group, key_part, preferred_element_type=jnp.float32)
            * score_scale
        )
        linked = jnp.any(link_group[:, :, :, None] == columns[None, None, None, :], axis=2)
        allowed = jnp.concatenate(
            [linked, jnp.ones((bundle, TILE, key_count - TILE), jnp.bool_)], axis=2
        )
        scores = jnp.where(allowed[:, None], scores, -1e30)
        highest = jnp.max(scores, axis=3, keepdims=True)
        weights = jnp.exp(scores - highest)
        total_rows = jnp.sum(weights, axis=3)
        blended = jnp.einsum(
            "bhqk,bkhd->bqhd",
            weights.astype(jnp.bfloat16),
            value_part,
            preferred_element_type=jnp.float32,
        )
        blended = blended / jnp.transpose(total_rows, (0, 2, 1))[..., None]
        return blended.astype(jnp.bfloat16).reshape(bundle * TILE, part_width)

    head_rows = lax.map(
        attend,
        (
            queries.reshape(group_count, bundle, TILE, head_count, head_size),
            key_value.reshape(group_count, bundle, TILE, 2 * part_width),
            neighbour_tiles.reshape(group_count, bundle, degree * TILE, 2 * part_width),
            local_nbr.reshape(group_count, bundle, TILE, local_nbr.shape[1]),
        ),
    ).reshape(row_count, part_width)
    rows_whole, virtual_whole, weight_whole = (
        lax.all_gather(head_rows, "rep", axis=1, tiled=True),
        lax.all_gather(virtual_heads, "rep", axis=1, tiled=True),
        lax.all_gather(w_out, "rep", axis=0, tiled=True),
    )
    own_start = lax.axis_index("rep") * part_width
    weight_cols = lax.dynamic_slice_in_dim(weight_whole, own_start, part_width, 1)
    node_sum = jnp.dot(rows_whole, weight_cols, preferred_element_type=jnp.float32)
    virtual_sum = jnp.dot(virtual_whole, weight_cols, preferred_element_type=jnp.float32)
    return (node_sum.astype(jnp.bfloat16), virtual_sum.astype(jnp.bfloat16))


MESH = pl.DeviceIdType.MESH
LOG2E = 1.4426950408889634
VPAD = 16
UNIT = 32
NEG = -1e30


def nt(a, b):
    return lax.dot_general(a, b, (((1,), (1,)), ((), ())), preferred_element_type=jnp.float32)


def nn(a, b):
    return lax.dot_general(a, b, (((1,), (0,)), ((), ())), preferred_element_type=jnp.float32)


def tn(a, b):
    return lax.dot_general(a, b, (((0,), (0,)), ((), ())), preferred_element_type=jnp.float32)


def fused(
    peers, reps, near_side, far_side,
    features, vstate, weights, tiles, links_in, out, vout,
    buf, wall, stage, vheads, links, vpad, top_ref, total_ref, acc_ref,
    own_sem, plane_recv, x_recv, core_recv, up_send, down_send, y_send, x_send, core_send,
    w_send, w_recv, o_send, o_recv, v_send, v_recv,
):
    units = features.shape[0]
    rows = units * UNIT
    half = units // 2
    width = features.shape[2] // reps
    head_size = D // H
    head_count = width // head_size
    coef = LOG2E / math.sqrt(head_size)
    blocks = rows // TILE // reps
    degree = tiles.shape[1]
    depth = peers // 2
    node, rep = lax.axis_index("nodes"), lax.axis_index("rep")
    z, y, x, core = node // 2, node % 2, rep // 2, rep % 2
    at_up, at_down = z < depth - 1, z > 0
    to_up, to_down = {"nodes": node + 2}, {"nodes": node - 2}
    to_y = {"nodes": z * 2 + (1 - y)}
    to_core, to_x, to_cross = (
        {"rep": x * 2 + (1 - core)},
        {"rep": (1 - x) * 2 + core},
        {"rep": (1 - x) * 2 + (1 - core)},
    )
    mates = (
        (to_core, x * 2 + (1 - core)),
        (to_x, (1 - x) * 2 + core),
        (to_cross, (1 - x) * 2 + (1 - core)),
    )

    own = pltpu.make_async_copy(features, buf.at[pl.ds(node * units, units)], own_sem.at[0])
    own_w = pltpu.make_async_copy(
        weights, wall.at[:, pl.ds(pl.multiple_of(rep * width, 16), width)], own_sem.at[1]
    )
    own_l = pltpu.make_async_copy(links_in, links, own_sem.at[2])
    own.start()
    own_w.start()
    own_l.start()

    barrier = pltpu.get_barrier_semaphore()
    for target in (to_y, to_core, to_x, to_cross):
        pl.semaphore_signal(barrier, inc=1, device_id=target, device_id_type=MESH)

    @pl.when(at_up)
    def _():
        pl.semaphore_signal(barrier, inc=1, device_id=to_up, device_id_type=MESH)

    @pl.when(at_down)
    def _():
        pl.semaphore_signal(barrier, inc=1, device_id=to_down, device_id_type=MESH)

    pl.semaphore_wait(barrier, 4 + at_up.astype(jnp.int32) + at_down.astype(jnp.int32))

    pending = []
    near_kinds, far_kinds = ("edge", "inner", "rest"), ("edge", "inner", "centre")
    slots = range(len(near_kinds))
    spans = {
        "edge": (0, near_side),
        "inner": (near_side, far_side - near_side),
        "rest": (far_side, half - near_side - far_side),
        "centre": (far_side, half - 2 * far_side),
    }

    def begin(which_core, kind, plane):
        start, size = spans[kind]
        return which_core * half + start + plane * (half - 2 * start - size), size

    def piece(chunk, which_core, kind, plane=x):
        start, size = begin(which_core, kind, plane)
        return buf.at[pl.ds(chunk * units + start, size)]

    def move(chunk, which_core, kind, send, recv, target, plane=x):
        ref = piece(chunk, which_core, kind, plane)
        return pltpu.make_async_remote_copy(
            src_ref=ref, dst_ref=ref, send_sem=send, recv_sem=recv, device_id=target, device_id_type=MESH
        )

    def under(cond, run):
        if cond is None:
            run()
        else:
            pl.when(cond)(run)

    def issue(cond, make):
        under(cond, lambda: make().start())
        pending.append((cond, make))

    def push(cond, sems, chunk, slot, kind, target):
        issue(cond, lambda: move(chunk, core, kind, sems.at[chunk, slot], plane_recv.at[chunk, slot], target))

    def push_own(cond, sems, slot, kind, target):
        def make():
            start, size = begin(core, kind, x)
            return pltpu.make_async_remote_copy(
                src_ref=features.at[pl.ds(start, size)], dst_ref=piece(node, core, kind),
                send_sem=sems.at[node, slot], recv_sem=plane_recv.at[node, slot],
                device_id=target, device_id_type=MESH,
            )

        issue(cond, make)

    def go_x(cond, chunk, slot):
        kind = near_kinds[slot]
        issue(cond, lambda: move(chunk, core, kind, x_send.at[chunk, slot], x_recv.at[chunk, slot], to_x))

    def go_core(cond, chunk, slot, kind, plane=x):
        issue(
            cond,
            lambda: move(
                chunk, core, kind, core_send.at[chunk, slot], core_recv.at[chunk, slot], to_core, plane
            ),
        )

    def wait_plane(cond, chunk, slot, kind):
        under(
            cond,
            lambda: move(chunk, core, kind, y_send.at[chunk, slot], plane_recv.at[chunk, slot], to_y).wait_recv(),
        )

    for slot in slots:
        push_own(at_up, up_send, slot, near_kinds[slot], to_up)
        push_own(at_down, down_send, slot, near_kinds[slot], to_down)
        push_own(None, y_send, slot, far_kinds[slot], to_y)
    own_w.wait()
    for index, (target, _) in enumerate(mates):
        wref = wall.at[:, pl.ds(pl.multiple_of(rep * width, 16), width)]
        issue(
            None,
            lambda wref=wref, index=index, target=target: pltpu.make_async_remote_copy(
                src_ref=wref, dst_ref=wref, send_sem=w_send.at[index], recv_sem=w_recv.at[rep],
                device_id=target, device_id_type=MESH,
            ),
        )

    lane = lax.broadcasted_iota(jnp.int32, (VPAD, 2 * width), 1)
    sub = lax.broadcasted_iota(jnp.int32, (VPAD, 2 * width), 0)
    kv_weight = jnp.concatenate([weights[1], weights[2]], axis=0)
    vpad[...] = jnp.zeros_like(vpad)
    vpad[:G] = vstate[...]
    virtual = vpad[...]
    vq = nt(virtual, jnp.concatenate([weights[0], weights[0]], axis=0)).astype(jnp.bfloat16).astype(jnp.float32)
    vq_rows = jnp.zeros((VPAD, 2 * width), jnp.float32)
    for h in range(head_count):
        moved = pltpu.roll(vq, h * G, 0) if h else vq
        keep = (lane >= h * head_size) & (lane < (h + 1) * head_size) & (sub >= h * G) & (sub < (h + 1) * G)
        vq_rows = jnp.where(keep, moved, vq_rows)
    vq_rows = vq_rows.astype(jnp.bfloat16)
    top_ref[...] = jnp.full((VPAD, 2 * width), NEG, jnp.float32)
    total_ref[...] = jnp.zeros((VPAD, 2 * width), jnp.float32)
    acc_ref[...] = jnp.zeros((VPAD, 2 * width), jnp.float32)

    def absorb(chunk):
        top = top_ref[:, :1]
        part = buf[pl.ds(chunk * units, units)].reshape(rows, D)
        kv = nt(part, kv_weight).astype(jnp.bfloat16)
        scores = nt(vq_rows, kv)
        new_top = jnp.maximum(top, jnp.max(scores, axis=1, keepdims=True))
        keep = jnp.exp2((top - new_top) * coef)
        w = jnp.exp2((scores - new_top) * coef)
        high = w.astype(jnp.bfloat16)
        low = (w - high.astype(jnp.float32)).astype(jnp.bfloat16)
        both = nn(jnp.concatenate([high, low], axis=0), kv)
        top_ref[...] = jnp.broadcast_to(new_top, (VPAD, 2 * width))
        total_ref[...] = total_ref[...] * keep + jnp.sum(w, axis=1, keepdims=True)
        acc_ref[...] = acc_ref[...] * keep + both[:VPAD] + both[VPAD:]

    own.wait()
    own_l.wait()
    absorb(node)

    def step_chunks(step, line):
        if step == 0:
            return [(None, z * 2 + line, None)]
        return [
            (z >= step, (z - step) * 2 + line, "up"),
            (z + step < depth, (z + step) * 2 + line, "down"),
        ]

    def groups(step):
        if step > 0:
            for cond, chunk, _ in step_chunks(step, y):
                yield cond, chunk, near_kinds, 1
        for cond, chunk, _ in step_chunks(step, 1 - y):
            yield cond, chunk, far_kinds, 2

    def x_arrivals(step):
        for slot in (0, 1):
            for cond, chunk, kinds, crossing in groups(step):
                if slot < crossing:
                    under(
                        cond,
                        lambda: move(
                            chunk, core, kinds[slot], x_send.at[chunk, slot], x_recv.at[chunk, slot], to_x, 1 - x
                        ).wait_recv(),
                    )
                    go_core(cond, chunk, len(slots) + slot, kinds[slot], 1 - x)

    def complete(step):
        for cond, chunk, kinds, crossing in groups(step):
            def run():
                for slot in range(len(slots) + crossing):
                    across = slot >= len(slots)
                    move(
                        chunk, 1 - core, kinds[slot - len(slots) if across else slot],
                        core_send.at[chunk, slot], core_recv.at[chunk, slot], to_core,
                        1 - x if across else x,
                    ).wait_recv()

            under(cond, run)

        def visit(i, carry):
            line, way = i % 2, i // 2
            place = z + (1 - 2 * way) * step
            fits = (place >= 0) & (place < depth)
            if step == 0:
                fits = i == 1 - y

            @pl.when(fits)
            def _():
                absorb(place * 2 + line)

            return carry

        lax.fori_loop(0, 2 if step == 0 else 4, visit, 0)

    for step in range(1, depth + 1):
        for slot in slots:
            if step < depth:
                for cond, chunk, way in step_chunks(step, y):
                    wait_plane(cond, chunk, slot, near_kinds[slot])
                    if way == "up":
                        push(cond & at_up, up_send, chunk, slot, near_kinds[slot], to_up)
                    else:
                        push(cond & at_down, down_send, chunk, slot, near_kinds[slot], to_down)
                    push(cond, y_send, chunk, slot, far_kinds[slot], to_y)
                    if slot == 0:
                        go_x(cond, chunk, slot)
                    go_core(cond, chunk, slot, near_kinds[slot])
            for cond, chunk, _ in step_chunks(step - 1, 1 - y):
                wait_plane(cond, chunk, slot, far_kinds[slot])
                if slot < 2:
                    go_x(cond, chunk, slot)
                go_core(cond, chunk, slot, far_kinds[slot])
        if step >= 2:
            x_arrivals(step - 2)
            complete(step - 2)
    x_arrivals(depth - 1)
    complete(depth - 1)

    for _, mate in mates:
        wref = wall.at[:, pl.ds(pl.multiple_of(mate * width, 16), width)]
        pltpu.make_async_remote_copy(
            src_ref=wref, dst_ref=wref, send_sem=w_send.at[0], recv_sem=w_recv.at[mate],
            device_id=to_core, device_id_type=MESH,
        ).wait_recv()

    acc, total = acc_ref[...], total_ref[...]
    acc = acc / total
    merged = jnp.zeros((VPAD, 2 * width), jnp.float32)
    for h in range(head_count):
        moved = pltpu.roll(acc, VPAD - h * G, 0) if h else acc
        keep = (lane >= width + h * head_size) & (lane < width + (h + 1) * head_size) & (sub < G)
        merged = jnp.where(keep, moved, merged)
    vheads[rep] = merged.astype(jnp.bfloat16)
    v_pending = []
    for index, (target, mate) in enumerate(mates):
        copy = pltpu.make_async_remote_copy(
            src_ref=vheads.at[rep], dst_ref=vheads.at[rep], send_sem=v_send.at[index],
            recv_sem=v_recv.at[rep], device_id=target, device_id_type=MESH,
        )
        copy.start()
        v_pending.append(copy)

    wq, wk, wv, wo = wall[0], wall[1], wall[2], wall[3]
    vk = nt(virtual, wk).astype(jnp.bfloat16)
    vvt = nt(wv, virtual).astype(jnp.bfloat16)
    dim_lane = lax.broadcasted_iota(jnp.int32, (TILE, D), 1)
    key_row = lax.broadcasted_iota(jnp.int32, (TILE, TILE), 0)
    pad_row = lax.broadcasted_iota(jnp.int32, (VPAD, 2 * TILE), 0)

    def out_copy(b, index, target, mate, slot):
        place = pl.multiple_of(slot * blocks * TILE + b * TILE, 16)
        return pltpu.make_async_remote_copy(
            src_ref=stage.at[b, mate], dst_ref=out.at[pl.ds(place, TILE)], send_sem=o_send.at[b, index],
            recv_sem=o_recv.at[b, slot], device_id=target, device_id_type=MESH,
        )

    def attend(b, carry):
        block = rep * blocks + b
        share = TILE // UNIT
        base = node * units + block * share
        parts = [buf[base + i] for i in range(share)]
        mine = jnp.concatenate(parts, axis=0)
        for j in range(degree):
            start = tiles[block, j] * share
            parts += [buf[start + i] for i in range(share)]
        source = jnp.concatenate(parts, axis=0)
        q = nt(mine, wq).astype(jnp.bfloat16)
        k = nt(source, wk).astype(jnp.bfloat16)
        vt = nt(wv, source).astype(jnp.bfloat16)
        lk = links[:, pl.ds(pl.multiple_of(block * TILE, TILE), TILE)]
        linked = key_row == lk[0:1, :]
        for i in range(1, links.shape[0]):
            linked = linked | (key_row == lk[i : i + 1, :])
        bias = jnp.where(linked, 0.0, NEG)
        bias = jnp.concatenate([bias, bias], axis=1)
        made = []
        for pair in range(H // 2):
            first = pair * 2
            qs = []
            for h in (first, first + 1):
                keep = (dim_lane >= h * head_size) & (dim_lane < (h + 1) * head_size)
                qs.append(jnp.where(keep, q, jnp.zeros_like(q)))
            qs = jnp.concatenate(qs, axis=0)
            s = nt(k, qs)
            sv = jnp.where(pad_row < G, nt(vk, qs), NEG)
            local = s[:TILE] + bias
            far = s[TILE:]
            highest = jnp.maximum(
                jnp.maximum(jnp.max(local, axis=0, keepdims=True), jnp.max(far, axis=0, keepdims=True)),
                jnp.max(sv, axis=0, keepdims=True),
            )
            wl = jnp.exp2((local - highest) * coef)
            wf = jnp.exp2((far - highest) * coef)
            ws = jnp.exp2((sv - highest) * coef)
            sums = (
                jnp.sum(wl, axis=0, keepdims=True)
                + jnp.sum(wf, axis=0, keepdims=True)
                + jnp.sum(ws, axis=0, keepdims=True)
            )
            w = jnp.concatenate([wl.astype(jnp.bfloat16), wf.astype(jnp.bfloat16)], axis=0)
            span = slice(first * head_size, (first + 2) * head_size)
            blend = nn(vt[span], w) + nn(vvt[span], ws.astype(jnp.bfloat16))
            blend = blend / sums
            made.append(blend[:head_size, :TILE])
            made.append(blend[head_size:, TILE:])
        head_t = jnp.concatenate(made, axis=0).astype(jnp.bfloat16)
        result = tn(head_t, wo).astype(jnp.bfloat16)
        for d in range(reps):
            stage[b, d] = result[:, d * width : (d + 1) * width]
        out[pl.ds(pl.multiple_of(rep * blocks * TILE + b * TILE, 16), TILE), :] = stage[b, rep]
        for index, (target, mate) in enumerate(mates):
            out_copy(b, index, target, mate, rep).start()
        return carry

    lax.fori_loop(0, blocks, attend, 0, unroll=2)

    for _, mate in mates:
        pltpu.make_async_remote_copy(
            src_ref=vheads.at[mate], dst_ref=vheads.at[mate], send_sem=v_send.at[0],
            recv_sem=v_recv.at[mate], device_id=to_core, device_id_type=MESH,
        ).wait_recv()
    for copy in v_pending:
        copy.wait_send()
    vsum = jnp.zeros((VPAD, D), jnp.float32)
    for d in range(reps):
        vsum = vsum + nn(vheads[d][:, width:], wo[d * width : (d + 1) * width])
    pick = vsum[:G, :width]
    for d in range(1, reps):
        pick = jnp.where(rep == d, vsum[:G, d * width : (d + 1) * width], pick)
    vout[...] = pick.astype(jnp.bfloat16)

    def finish(b, carry):
        for index, (target, mate) in enumerate(mates):
            out_copy(b, index, target, mate, rep).wait_send()
            out_copy(b, index, target, mate, mate).wait_recv()
        return carry

    lax.fori_loop(0, blocks, finish, 0)
    for cond, make in pending:
        under(cond, lambda: make().wait_send())


def gathered(peers, reps, features, virtual_state, w_query, w_key, w_value, w_out, tile_map, local_nbr):
    rows = features.shape[0]
    width = w_query.shape[1]
    half = rows // UNIT // 2
    near_side = half * 10 // 32
    far_side = half * 11 // 32
    weights = jnp.stack([w_query.T, w_key.T, w_value.T, w_out])
    blocks = rows // TILE // reps
    dma = pltpu.SemaphoreType.DMA
    vmem = pl.BlockSpec(memory_space=pltpu.VMEM)
    return pl.pallas_call(
        functools.partial(fused, peers, reps, near_side, far_side),
        out_shape=(
            jax.ShapeDtypeStruct((rows, width), jnp.bfloat16),
            jax.ShapeDtypeStruct((G, width), jnp.bfloat16),
        ),
        in_specs=[
            pl.BlockSpec(memory_space=pl.ANY), vmem, vmem,
            pl.BlockSpec(memory_space=pltpu.SMEM), pl.BlockSpec(memory_space=pl.ANY),
        ],
        out_specs=(vmem, vmem),
        scratch_shapes=[
            pltpu.VMEM((peers * rows // UNIT, UNIT, D), jnp.bfloat16),
            pltpu.VMEM((4, D, D), jnp.bfloat16),
            pltpu.VMEM((blocks, reps, TILE, width), jnp.bfloat16),
            pltpu.VMEM((reps, VPAD, 2 * width), jnp.bfloat16),
            pltpu.VMEM(local_nbr.shape[::-1], jnp.int32),
            pltpu.VMEM((VPAD, D), jnp.bfloat16),
            pltpu.VMEM((VPAD, 2 * width), jnp.float32),
            pltpu.VMEM((VPAD, 2 * width), jnp.float32),
            pltpu.VMEM((VPAD, 2 * width), jnp.float32),
            dma((3,)), dma((peers, 3)), dma((peers, 2)), dma((peers, 5)),
            dma((peers, 3)), dma((peers, 3)), dma((peers, 3)), dma((peers, 2)), dma((peers, 5)),
            dma((3,)), dma((reps,)), dma((blocks, 3)), dma((blocks, reps)), dma((3,)), dma((reps,)),
        ],
        compiler_params=pltpu.CompilerParams(
            collective_id=0, has_side_effects=True, vmem_limit_bytes=48 * 1024 * 1024
        ),
        name="exphormer",
    )(features.reshape(rows // UNIT, UNIT, D), virtual_state, weights, tile_map, local_nbr.T)


def solution(mesh):
    peers, reps = mesh.shape["nodes"], mesh.shape["rep"]

    def local(features, *rest):
        fits = peers * features.size * 2 <= 16 * 1024 * 1024
        if fits and reps == 4 and peers % 2 == 0:
            return gathered(peers, reps, features, *rest)
        return shards(features, *rest)

    in_specs = (
        P("nodes", None),
        P(),
        P(None, "rep"),
        P(None, "rep"),
        P(None, "rep"),
        P("rep", None),
        P("nodes", None),
        P("nodes", None),
    )
    out_specs = (P("nodes", "rep"), P(None, "rep"))
    return jax.shard_map(local, mesh=mesh, in_specs=in_specs, out_specs=out_specs, check_vma=False)
```
